32 devices in a mesh: segment: 2 (over core), dp: 4 (over z), mp: 4 (over y, x).
Axes of the slice: x: 2, y: 2, z: 4, core: 2. Of those that a mesh axis runs over, the one named last changes fastest.
Arguments:
- candidates: bfloat16 [2048, 4096], P(('segment', 'dp'), 'mp'), may hold values from -6 to 6
- scorer_value: bfloat16 [2, 4096, 1024], P('segment', 'mp'), may hold values from -0.09375 to 0.09375
- scorer_out: bfloat16 [2, 1024, 4096], P('segment', None, 'mp'), may hold values from -0.1875 to 0.1875
- learner_value: bfloat16 [2, 4096, 1024], P('segment', 'mp'), may hold values from -0.0625 to 0.0625
- learner_out: bfloat16 [2, 1024, 4096], P('segment', None, 'mp'), may hold values from -0.1875 to 0.1875
- keep_index: int32 [8, 128], P(('segment', 'dp')), may hold values from 0 to 255, as said below
- keep_dest: int32 [8, 128], P(('segment', 'dp')), may hold values from 0 to 3, as said below
- keep_count: int32 [8], P(('segment', 'dp')), may hold values from 64 to 128, as said below
Outputs:
- grad_value: float32 [2, 1024, 4096], P('segment', 'dp', 'mp')
- grad_out: float32 [2, 1024, 4096], P('segment', 'dp', 'mp')
The draws below stay inside these ranges and needn't reach their ends.
Inputs may be any that keep to these rules, and one draw needn't show every extreme that they name: `keep_index`: the entries of one shard's list are distinct. `keep_dest`: no candidate shard sends more than 64 of its first keep_count kept tokens to one learner shard, and some shard sends exactly 64; every learner shard receives at least one kept token from its own segment. Entries of keep_index and keep_dest at positions keep_count or later are ignored.
All inputs are finite; a program needn't handle non-finite values.
Results may differ from the reference program's by a relative error of at most 0.008.
Values may be sent and summed in bfloat16 or wider, within the bound.
No kernel may reach another device: no remote copies, remote signals or barrier semaphores. Data moves between devices by JAX's collectives and lax.ppermute only.
A program may use at most 128 MiB of HBM per device.

```python
import jax
import jax.numpy as jnp
from jax import lax

DS = 4096
KVS = 1024
DL = 8192
KVL = 1024
CH = 256
KEEP = 128
CAND = 2048
N_SEGMENT = 2
N_DP = 4


def routing_tables(key):
    base_key = jax.random.fold_in(key, 11)
    key_count, key_top, key_perm, key_rank, key_score = jax.random.split(base_key, 5)
    shards = N_SEGMENT * N_DP
    counts = jax.random.randint(key_count, (shards,), KEEP // 2, KEEP + 1)
    top_shard = jax.random.randint(key_top, (), 0, shards)
    counts = jnp.where(jnp.arange(shards) == top_shard, KEEP, counts)
    jitter = jax.random.randint(key_perm, (shards, CH), 0, 1 << 20)
    shuffled = jnp.argsort(jitter * CH + jnp.arange(CH)[None, :], axis=1)
    kept_index = shuffled[:, :KEEP].astype(jnp.int32)
    tickets = 2 * KEEP
    per_slot = tickets // N_DP
    rank_jitter = jax.random.randint(key_rank, (N_DP,), 0, 1 << 20)
    dest_rank = jnp.argsort(jnp.argsort(rank_jitter * N_DP + jnp.arange(N_DP)))
    ticket = jnp.arange(tickets)
    ticket_dest = ticket // per_slot
    ticket_rank = dest_rank[ticket_dest]
    priority = ticket_rank * (65536 // N_DP)
    priority = jnp.where(ticket_rank == N_DP - 1, 2 * 65536, priority)
    own_dp = (jnp.arange(shards) % N_DP)[:, None]
    own_ticket = (ticket_dest[None, :] == own_dp) & (ticket[None, :] % per_slot == 0)
    priority = jnp.where(own_ticket, 3 * 65536, priority[None, :])
    scores = jax.random.randint(key_score, (shards, tickets), 0, 65536) + priority
    picked = jnp.argsort(-(scores * tickets + ticket[None, :]), axis=1)[:, :KEEP]
    kept_dest = (picked // per_slot).astype(jnp.int32)
    return (kept_index, kept_dest, counts.astype(jnp.int32))


def draw_keep_index(key, part):
    return routing_tables(key)[0]


def draw_keep_dest(key, part):
    return routing_tables(key)[1]


def draw_keep_count(key, part):
    return routing_tables(key)[2]


def shard_levels(own_key, extent, cuts, smallest, largest):
    level = 1.0
    for dim, shards_of in cuts:
        heights = jax.random.uniform(jax.random.fold_in(jax.random.fold_in(own_key, 6), dim), (shards_of,), jnp.float32, smallest / len(cuts), largest / len(cuts))
        level = level * jnp.repeat(jnp.exp(heights), extent[dim] // shards_of).reshape((-1,) + (1,) * (len(extent) - 1 - dim))
    return level


def scatter_about(stream_key, extent, width, reach, cuts=(), kind=jnp.bfloat16):
    entries = jax.random.normal(stream_key, extent, jnp.float32) * width
    if len(cuts) > 0:
        entries = shard_levels(stream_key, extent, cuts, -0.22, 0.18) * entries
    return jnp.clip(entries, min=-reach, max=reach).astype(kind)


def setup_inputs(seed: int = 0) -> dict:
    key_of = jax.random.split(jax.random.key(seed), 9)
    candidates = scatter_about(key_of[0], (CAND, DS), 1.0, 6.0, ((0, 8), (1, 4)))
    scorer_value = scatter_about(key_of[1], (N_SEGMENT, DS, KVS), DS ** -0.5, 0.09375, ((0, 2), (1, 4)))
    scorer_out = scatter_about(key_of[2], (N_SEGMENT, KVS, DS), KVS ** -0.5, 0.1875, ((0, 2), (2, 4)))
    learner_value = scatter_about(key_of[3], (N_SEGMENT, DS, KVL), DL ** -0.5, 0.0625, ((0, 2), (1, 4)))
    learner_out = scatter_about(key_of[4], (N_SEGMENT, KVL, DS), KVL ** -0.5, 0.1875, ((0, 2), (2, 4)))
    keep_index = draw_keep_index(jax.random.fold_in(key_of[8], 71), 0)
    keep_dest = draw_keep_dest(jax.random.fold_in(key_of[8], 71), 0)
    keep_count = draw_keep_count(jax.random.fold_in(key_of[8], 71), 0)
    return {"candidates": candidates, "scorer_value": scorer_value, "scorer_out": scorer_out, "learner_value": learner_value, "learner_out": learner_out, "keep_index": keep_index, "keep_dest": keep_dest, "keep_count": keep_count}


EPSILON = 1e-05

def section(hidden, w_value, w_out):
    widened = hidden.astype(jnp.float32)
    squares = lax.optimization_barrier(jnp.sum(widened * widened, axis=1))
    inverse = lax.rsqrt(squares / hidden.shape[1] + EPSILON)
    values = (jnp.dot(hidden, w_value, preferred_element_type=jnp.float32) * inverse[:, None]).astype(jnp.bfloat16)
    return (widened + jnp.dot(values, w_out, preferred_element_type=jnp.float32)).astype(jnp.bfloat16)

def reference(candidates, scorer_value, scorer_out, learner_value, learner_out, keep_index, keep_dest, keep_count):
    middle = section(candidates, scorer_value[0], scorer_out[0])
    scored = section(middle, scorer_value[1], scorer_out[1])
    shard_total = keep_index.shape[0]
    is_live = (jnp.arange(KEEP, dtype=jnp.int32)[None, :] < keep_count[:, None]).reshape(-1)
    row_ids = (keep_index + (jnp.arange(shard_total, dtype=jnp.int32) * CH)[:, None]).reshape(-1)
    inputs = jnp.concatenate([candidates[row_ids], scored[row_ids]], axis=1)
    inputs = jnp.where(is_live[:, None], inputs, jnp.zeros((), inputs.dtype))
    segment_ids = jnp.arange(shard_total, dtype=jnp.int32) // N_DP
    learner_ids = (segment_ids[:, None] * N_DP + keep_dest).reshape(-1)
    one_hot = (learner_ids[:, None] == jnp.arange(shard_total, dtype=jnp.int32)[None, :]) & is_live[:, None]
    shard_counts = lax.optimization_barrier(jnp.sum(one_hot.astype(jnp.float32), axis=0))
    row_counts = shard_counts[learner_ids]
    widened = inputs.astype(jnp.float32)
    squares = lax.optimization_barrier(jnp.sum(widened * widened, axis=1))
    inverse = lax.rsqrt(squares / DL + EPSILON)
    value_map = learner_value.reshape(DL, KVL)
    out_map = jnp.transpose(learner_out, (1, 0, 2)).reshape(KVL, DL)
    values = (jnp.dot(inputs, value_map, preferred_element_type=jnp.float32) * inverse[:, None]).astype(jnp.bfloat16)
    normed = (widened * inverse[:, None]).astype(jnp.bfloat16)
    output = widened + jnp.dot(values, out_map, preferred_element_type=jnp.float32)
    slopes = (output / row_counts[:, None]).astype(jnp.bfloat16)
    back = jnp.dot(slopes, out_map.T, preferred_element_type=jnp.float32).astype(jnp.bfloat16)
    grad_value = jnp.dot(back.T, normed, preferred_element_type=jnp.float32)
    grad_out = jnp.dot(values.T, slopes, preferred_element_type=jnp.float32)
    grad_value = jnp.transpose(grad_value.reshape(KVL, 2, DS), (1, 0, 2))
    grad_out = jnp.transpose(grad_out.reshape(KVL, 2, DS), (1, 0, 2))
    return (grad_value, grad_out)
```

```python
import jax
import jax.numpy as jnp
from jax import lax
from jax.sharding import PartitionSpec as P

EPSILON = 1e-05
BF = jnp.bfloat16
F32 = jnp.float32
SIDE = 128


def flip(value, axis, mask):
    pairs = [(source, source ^ mask) for source in range(lax.axis_size(axis))]
    return lax.ppermute(value, axis, pairs)


def matmul(left, right):
    return jnp.dot(left, right, preferred_element_type=F32)


def matmul_nt(left, right):
    return lax.dot_general(left, right, (((1,), (1,)), ((), ())), preferred_element_type=F32)


def matmul_tn(left, right):
    return lax.dot_general(left, right, (((0,), (0,)), ((), ())), preferred_element_type=F32)


def pack(columns):
    lane = lax.broadcasted_iota(jnp.int32, (columns[0].shape[0], SIDE), 1)
    side = jnp.zeros(lane.shape, F32)
    for place, column in enumerate(columns):
        rest = column
        for part in range(3):
            piece = lax.reduce_precision(rest, 8, 7)
            side = jnp.where(lane == 3 * place + part, piece, side)
            rest = rest - piece
    return side.astype(BF)


def unpack(side, place):
    wide = side[:, 3 * place : 3 * place + 3].astype(F32)
    return wide[:, 0:1] + wide[:, 1:2] + wide[:, 2:3]


def square_sum(value):
    wide = value.astype(F32)
    return jnp.sum(wide * wide, axis=1, keepdims=True)


def reduce_rows(partial, squares):
    half = partial.shape[0] // 2
    width = partial.shape[1]

    def step(part, norm, mask):
        sent = jnp.concatenate([part.astype(BF), pack([norm])], axis=1)
        got = flip(sent, "mp", mask)
        return part + got[:, :width].astype(F32), norm + unpack(got[:, width:], 0)

    top, top_norm = step(partial[:half], squares[:half], 1)
    low, low_norm = step(partial[half:], squares[half:], 2)
    top, top_norm = step(top, top_norm, 2)
    low, low_norm = step(low, low_norm, 1)
    return (
        jnp.concatenate([top, low], axis=0),
        jnp.concatenate([top_norm, low_norm], axis=0),
    )


def on_device(
    candidates,
    scorer_value,
    scorer_out,
    learner_value,
    learner_out,
    keep_index,
    keep_dest,
    keep_count,
):
    first = lax.axis_index("segment") == 0
    dp_at = lax.axis_index("dp")
    mp_at = lax.axis_index("mp")
    dp_size = lax.axis_size("dp")
    mp_size = lax.axis_size("mp")
    keep = keep_index.shape[1]
    width = candidates.shape[1]
    scorer_width = width * mp_size
    learner_width = 2 * scorer_width
    inner = learner_value.shape[2]
    block = inner // dp_size
    share = keep // mp_size

    own_value, own_out = scorer_value[0], scorer_out[0]
    own_lvalue, own_lout = learner_value[0], learner_out[0]
    other_value = flip(own_value, "segment", 1)
    other_out = flip(own_out, "segment", 1)
    other_lvalue = flip(own_lvalue, "segment", 1)
    other_lout = flip(own_lout, "segment", 1)

    is_live = jnp.arange(keep) < keep_count[0]
    pick = (keep_index[0][:, None] == jnp.arange(candidates.shape[0])[None, :]) & is_live[:, None]
    rows = matmul(pick.astype(BF), candidates).astype(BF)
    to_peer = (keep_dest[0][:, None] == jnp.arange(dp_size)[None, :]) & is_live[:, None]
    marked = to_peer.astype(jnp.int32)
    own_counts = jnp.sum(marked, axis=0, keepdims=True)
    counts = own_counts
    for mask in range(1, dp_size):
        counts = counts + flip(own_counts, "dp", mask)
    token_count = jnp.sum(marked * counts, axis=1, keepdims=True)
    token_count = jnp.where(is_live[:, None], token_count, 1).astype(F32)

    rows_squares = square_sum(rows)
    nothing = jnp.zeros_like(rows)
    partial = matmul(jnp.where(first, rows, nothing), own_value) + matmul(
        jnp.where(first, nothing, rows), other_value
    )
    hidden = rows
    squares = rows_squares
    for index in range(2):
        total, norm = reduce_rows(partial, squares)
        inverse = lax.rsqrt(norm / scorer_width + EPSILON)
        values = (total * inverse).astype(BF)
        if index == 0:
            w_out = lax.optimization_barrier(jnp.where(first, own_out, other_out))
        else:
            w_out = lax.optimization_barrier(jnp.where(first, other_out, own_out))
        hidden = (hidden.astype(F32) + matmul(values, w_out)).astype(BF)
        squares = square_sum(hidden)
        if index == 0:
            w_value = lax.optimization_barrier(jnp.where(first, other_value, own_value))
            partial = matmul(hidden, w_value)
    scored = hidden

    gram = matmul_nt(own_lout, lax.dynamic_slice_in_dim(own_lout, dp_at * block, block, 0))
    half = inner // 2
    at = lax.axis_index("segment")
    kept_half = lax.dynamic_slice_in_dim(gram, at * half, half, 0)
    sent_half = lax.dynamic_slice_in_dim(gram, (1 - at) * half, half, 0)
    kept_half = kept_half + flip(sent_half.astype(BF), "segment", 1).astype(F32)
    top, low = kept_half[: half // 2], kept_half[half // 2 :]
    top, low = (
        top + flip(top.astype(BF), "mp", 1).astype(F32),
        low + flip(low.astype(BF), "mp", 2).astype(F32),
    )
    top, low = (
        top + flip(top.astype(BF), "mp", 2).astype(F32),
        low + flip(low.astype(BF), "mp", 1).astype(F32),
    )
    gram_half = jnp.concatenate([top, low], axis=0).astype(BF)
    gram_other = flip(gram_half, "segment", 1)
    gram = jnp.where(
        first,
        jnp.concatenate([gram_half, gram_other], axis=0),
        jnp.concatenate([gram_other, gram_half], axis=0),
    )

    own_x = jnp.where(first, rows, scored)
    other_x = jnp.where(first, scored, rows)
    partial = jnp.concatenate(
        [
            matmul(own_x, own_lvalue) + matmul(other_x, other_lvalue),
            matmul_nt(own_x, own_lout) + matmul_nt(other_x, other_lout),
        ],
        axis=1,
    )
    squares = rows_squares + squares

    def share_of(array, peer):
        return lax.dynamic_slice_in_dim(array, peer * share, share, 0)

    sent = jnp.concatenate([partial.astype(BF), pack([squares])], axis=1)
    total, norm = share_of(partial, mp_at), share_of(squares, mp_at)
    for mask in range(1, mp_size):
        got = flip(share_of(sent, mp_at ^ mask), "mp", mask)
        total = total + got[:, : 2 * inner].astype(F32)
        norm = norm + unpack(got[:, 2 * inner :], 0)
    inverse = lax.rsqrt(norm / learner_width + EPSILON)
    values = (total[:, :inner] * inverse).astype(BF)
    crossed = total[:, inner:].astype(BF)
    side = pack([inverse, share_of(token_count, mp_at)])

    def in_order(array):
        return jnp.concatenate([share_of(array, mp_at ^ mask) for mask in range(mp_size)], axis=0)

    rows_order, scored_order = in_order(rows), in_order(scored)
    column = dp_at * block

    def add(grads, piece, near_rows, near_scored):
        shares = [piece] + [flip(piece, "mp", mask) for mask in range(1, mp_size)]
        tokens = jnp.concatenate(shares, axis=0)
        tokens = jnp.concatenate([tokens, flip(tokens, "segment", 1)], axis=0)
        near = jnp.where(first, near_rows, near_scored)
        far = flip(jnp.where(first, near_scored, near_rows), "segment", 1)
        x = jnp.concatenate([near, far], axis=0).astype(F32)
        v = tokens[:, :inner]
        xo = tokens[:, inner : inner + block].astype(F32)
        scalars = tokens[:, inner + block :]
        inv = unpack(scalars, 0)
        share_count = 1.0 / unpack(scalars, 1)
        slopes = ((x + matmul(v, own_lout)) * share_count).astype(BF)
        normed = (x * inv).astype(BF)
        back = ((xo + matmul(v, gram)) * share_count).astype(BF)
        v_block = lax.dynamic_slice_in_dim(v, column, block, 1)
        return (grads[0] + matmul_tn(back, normed), grads[1] + matmul_tn(v_block, slopes))

    grads = (jnp.zeros((block, width), F32), jnp.zeros((block, width), F32))
    if dp_size <= 8:
        for away in range(dp_size):
            cross = lax.dynamic_slice_in_dim(crossed, (dp_at ^ away) * block, block, 1)
            piece = jnp.concatenate([values, cross, side], axis=1)
            near_rows, near_scored = rows_order, scored_order
            if away > 0:
                piece = flip(piece, "dp", away)
                near_rows = flip(rows_order, "dp", away)
                near_scored = flip(scored_order, "dp", away)
            grads = add(grads, piece, near_rows, near_scored)
    else:
        ring = [(source, (source + 1) % dp_size) for source in range(dp_size)]

        def turn(_, carry):
            grads, held = carry
            full, near_rows, near_scored = held
            cross = lax.dynamic_slice_in_dim(full, inner + column, block, 1)
            piece = jnp.concatenate([full[:, :inner], cross, full[:, 2 * inner :]], axis=1)
            grads = add(grads, piece, near_rows, near_scored)
            return grads, [lax.ppermute(array, "dp", ring) for array in held]

        full = jnp.concatenate([values, crossed, side], axis=1)
        grads, _ = lax.fori_loop(0, dp_size, turn, (grads, [full, rows_order, scored_order]))
    grad_value, grad_out = grads
    return (grad_value[None], grad_out[None])


def solution(mesh):
    placed = (
        P(("segment", "dp"), "mp"),
        P("segment", "mp", None),
        P("segment", None, "mp"),
        P("segment", "mp", None),
        P("segment", None, "mp"),
        P(("segment", "dp"), None),
        P(("segment", "dp"), None),
        P(("segment", "dp")),
    )
    return jax.shard_map(
        on_device,
        mesh=mesh,
        in_specs=placed,
        out_specs=(P("segment", "dp", "mp"), P("segment", "dp", "mp")),
        check_vma=False,
    )
```

```python
import functools

import jax
import jax.numpy as jnp
from jax import lax
from jax.experimental import pallas as pl
from jax.experimental.pallas import tpu as pltpu
from jax.sharding import PartitionSpec as P

EPSILON = 1e-05
BF = jnp.bfloat16
F32 = jnp.float32
SIDE = 128


def flip(value, axis, mask):
    pairs = [(source, source ^ mask) for source in range(lax.axis_size(axis))]
    return lax.ppermute(value, axis, pairs)


def matmul(left, right):
    return jnp.dot(left, right, preferred_element_type=F32)


def matmul_nt(left, right):
    return lax.dot_general(left, right, (((1,), (1,)), ((), ())), preferred_element_type=F32)


def matmul_tn(left, right):
    return lax.dot_general(left, right, (((0,), (0,)), ((), ())), preferred_element_type=F32)


def pack(columns):
    lane = lax.broadcasted_iota(jnp.int32, (columns[0].shape[0], SIDE), 1)
    side = jnp.zeros(lane.shape, F32)
    for place, column in enumerate(columns):
        rest = column
        for part in range(3):
            piece = lax.reduce_precision(rest, 8, 7)
            side = jnp.where(lane == 3 * place + part, piece, side)
            rest = rest - piece
    return side.astype(BF)


def unpack(side, place):
    wide = side[:, 3 * place : 3 * place + 3].astype(F32)
    return wide[:, 0:1] + wide[:, 1:2] + wide[:, 2:3]


VMEM = pl.BlockSpec(memory_space=pltpu.VMEM)
SMEM = pl.BlockSpec(memory_space=pltpu.SMEM)
HBM = pl.BlockSpec(memory_space=pl.ANY)


def call(body, outs, in_specs, scratch=()):
    return pl.pallas_call(
        body,
        out_shape=outs,
        in_specs=in_specs,
        out_specs=jax.tree.map(lambda _: VMEM, outs),
        scratch_shapes=list(scratch),
        compiler_params=pltpu.CompilerParams(vmem_limit_bytes=48 << 20),
    )


def side_of(column):
    lane = lax.broadcasted_iota(jnp.int32, (column.shape[0], SIDE), 1)
    high = column.astype(BF).astype(F32)
    middle = (column - high).astype(BF).astype(F32)
    low = column - high - middle
    zero = jnp.zeros(lane.shape, F32)
    picked = jnp.where(lane == 0, high, jnp.where(lane == 1, middle, jnp.where(lane == 2, low, zero)))
    return picked.astype(BF)


def from_side(side):
    return jnp.sum(side.astype(F32), axis=1, keepdims=True)


def learn_kernel(features, share, where, total, norm, middle, rows, rows_squares, *refs):
    (out_a, out_b, value_a, value_b, lout_a, lout_b) = refs[:6]
    scored, kept, kept_norm = refs[6:9]
    peers, chosen, sent = refs[9:-2], refs[-2], refs[-1]
    first, at = where[0] == 1, where[1]
    values = (total[...] * lax.rsqrt(norm[...] / features + EPSILON)).astype(BF)

    @pl.when(first)
    def _():
        chosen[...] = matmul(values, out_b[...])

    @pl.when(jnp.logical_not(first))
    def _():
        chosen[...] = matmul(values, out_a[...])

    row = rows[...]
    score = (middle[...].astype(F32) + chosen[...]).astype(BF)
    scored[...] = score
    squares = rows_squares[...] + square_sum(score)
    own = jnp.where(first, row, score)
    other = jnp.where(first, score, row)
    inner = value_a.shape[1]
    part = matmul(own, value_a[...]) + matmul(other, value_b[...])
    cross = matmul_nt(own, lout_a[...]) + matmul_nt(other, lout_b[...])
    side = side_of(squares)
    sent[:, :inner] = part
    sent[:, inner : 2 * inner] = cross
    sent[:, 2 * inner :] = side.astype(F32)
    mine = sent[pl.ds(pl.multiple_of(at * share, share), share), :]
    kept[...] = mine[:, : 2 * inner]
    kept_norm[...] = from_side(mine[:, 2 * inner :])
    for place, peer in enumerate(peers):
        start = pl.multiple_of((at ^ (place + 1)) * share, share)
        peer[...] = sent[pl.ds(start, share), :].astype(BF)


def value_kernel(features, block, count, where, kept, norm, *refs):
    got, pieces, crossed = refs[:count], refs[count:-1], refs[-1]
    total, squares = kept[...], norm[...]
    inner = total.shape[1] // 2
    for one in got:
        total = total + one[:, : 2 * inner].astype(F32)
        squares = squares + from_side(one[:, 2 * inner :])
    inverse = lax.rsqrt(squares / features + EPSILON)
    values = (total[:, :inner] * inverse).astype(BF)
    side = side_of(inverse)
    crossed[...] = total[:, inner:].astype(BF)
    for away, piece in enumerate(pieces):
        if len(pieces) == 1:
            cross = crossed[...]
        else:
            cross = crossed[:, pl.ds(pl.multiple_of((where[0] ^ away) * block, block), block)]
        reach = inner + cross.shape[1]
        piece[:, :inner] = values
        piece[:, inner:reach] = cross
        piece[:, reach:] = side


def gradient_kernel(share, peers, dp_size, where, *refs):
    count = 4 * peers
    near, far = refs[:count:2], refs[1:count:2]
    every_row, every_scored, parts, lout, gram, grad_value, grad_out = refs[count : count + 7]
    tokens, x, slopes, normed, back, token_sem, x_sem = refs[count + 7 :]
    first, dp_at, mp_at = where[0] == 1, where[1], where[2]
    keep = share * peers
    width, inner, block = x.shape[1], lout.shape[0], gram.shape[1]
    piece = inner + block + SIDE

    def x_copy(source):
        return pltpu.make_async_copy(source, x, x_sem)

    @pl.when(first)
    def _():
        x_copy(every_row.at[:, pl.ds(0, width)]).start()

    @pl.when(jnp.logical_not(first))
    def _():
        x_copy(every_scored).start()

    copies = []
    for side, group in enumerate((near, far)):
        segment = jnp.where(first, side, 1 - side)
        for mask in range(peers):
            own, rest = group[mask], group[peers + mask]
            for away in range(dp_size):
                source = own if away == 0 else rest.at[:, pl.ds((away - 1) * piece, piece)]
                start = ((segment * dp_size + (dp_at ^ away)) * peers + (mp_at ^ mask)) * share
                target = tokens.at[pl.ds(pl.multiple_of(start, share), share), :]
                copy = pltpu.make_async_copy(source, target, token_sem.at[len(copies)])
                copy.start()
                copies.append(copy)
    for copy in copies:
        copy.wait()
    x_copy(every_scored).wait()
    step = 2 * keep
    for at in range(0, tokens.shape[0], step):
        here = pl.ds(at, step)
        wide = x[here, :].astype(F32)
        values = tokens[here, :inner]
        share_count = parts[here, :]
        inverse = from_side(tokens[here, inner + block :])
        slopes[here, :] = ((wide + matmul(values, lout[...])) * share_count).astype(BF)
        normed[here, :] = (wide * inverse).astype(BF)
        crossed = tokens[here, inner : inner + block].astype(F32)
        back[here, :] = ((crossed + matmul(values, gram[...])) * share_count).astype(BF)
    grad_value[...] = matmul_tn(back[...], normed[...])
    column = pl.multiple_of(dp_at * block, block)
    grad_out[...] = matmul_tn(tokens[:, pl.ds(column, block)], slopes[...])


def square_sum(value):
    wide = value.astype(F32)
    return jnp.sum(wide * wide, axis=1, keepdims=True)


def exchange(first, second, first_mask, second_mask):
    first, second = lax.optimization_barrier((first, second))
    return lax.optimization_barrier(
        (flip(first, "mp", first_mask), flip(second, "mp", second_mask))
    )


def reduce_rows(partial, squares):
    half = partial.shape[0] // 2
    width = partial.shape[1]

    def sent(part, norm):
        return jnp.concatenate([part.astype(BF), pack([norm])], axis=1)

    top, low = (partial[:half], squares[:half]), (partial[half:], squares[half:])
    for top_mask, low_mask in ((1, 2), (2, 1)):
        got = exchange(sent(*top), sent(*low), top_mask, low_mask)
        top, low = (
            (part + new[:, :width].astype(F32), norm + unpack(new[:, width:], 0))
            for (part, norm), new in zip((top, low), got)
        )
    return (
        jnp.concatenate([top[0], low[0]], axis=0),
        jnp.concatenate([top[1], low[1]], axis=0),
    )


def on_device(
    candidates,
    scorer_value,
    scorer_out,
    learner_value,
    learner_out,
    keep_index,
    keep_dest,
    keep_count,
):
    first = lax.axis_index("segment") == 0
    dp_at = lax.axis_index("dp")
    mp_at = lax.axis_index("mp")
    dp_size = lax.axis_size("dp")
    mp_size = lax.axis_size("mp")
    keep = keep_index.shape[1]
    width = candidates.shape[1]
    scorer_width = width * mp_size
    learner_width = 2 * scorer_width
    inner = learner_value.shape[2]
    block = inner // dp_size
    share = keep // mp_size

    own_value, own_out = scorer_value[0], scorer_out[0]
    own_lvalue, own_lout = learner_value[0], learner_out[0]
    other_value = flip(own_value, "segment", 1)
    other_out = flip(own_out, "segment", 1)
    other_lvalue = flip(own_lvalue, "segment", 1)
    other_lout = flip(own_lout, "segment", 1)

    is_live = jnp.arange(keep) < keep_count[0]
    pick = (keep_index[0][:, None] == jnp.arange(candidates.shape[0])[None, :]) & is_live[:, None]
    rows = matmul(pick.astype(BF), candidates).astype(BF)
    goal = jnp.where(is_live, keep_dest[0] + 1, 0).astype(F32)[:, None]
    every_row = lax.all_gather(
        jnp.concatenate([rows, jnp.broadcast_to(goal, (keep, SIDE)).astype(BF)], axis=1),
        ("segment", "dp"),
        axis=0,
        tiled=False,
    )

    gram = matmul_nt(own_lout, lax.dynamic_slice_in_dim(own_lout, dp_at * block, block, 0))
    half = inner // 2
    at = lax.axis_index("segment")
    kept_half = lax.dynamic_slice_in_dim(gram, at * half, half, 0)
    sent_half = lax.dynamic_slice_in_dim(gram, (1 - at) * half, half, 0)
    half_sum = (kept_half + flip(sent_half.astype(BF), "segment", 1).astype(F32)).astype(BF)
    gram_parts = lax.all_gather(half_sum, "mp", axis=0, tiled=False)

    rows_squares = square_sum(rows)
    nothing = jnp.zeros_like(rows)
    partial = matmul(jnp.where(first, rows, nothing), own_value) + matmul(
        jnp.where(first, nothing, rows), other_value
    )
    total, norm = reduce_rows(partial, rows_squares)
    inverse = lax.rsqrt(norm / scorer_width + EPSILON)
    values = (total * inverse).astype(BF)
    w_out = lax.optimization_barrier(jnp.where(first, own_out, other_out))
    middle = (rows.astype(F32) + matmul(values, w_out)).astype(BF)
    w_value = lax.optimization_barrier(jnp.where(first, other_value, own_value))
    total, norm = reduce_rows(matmul(middle, w_value), square_sum(middle))
    total, every_row = lax.optimization_barrier((total, every_row))

    flag = first.astype(jnp.int32)
    long = 2 * inner + SIDE
    outs = call(
        functools.partial(learn_kernel, scorer_width, share),
        [
            jax.ShapeDtypeStruct((keep, width), BF),
            jax.ShapeDtypeStruct((share, 2 * inner), F32),
            jax.ShapeDtypeStruct((share, 1), F32),
        ]
        + [jax.ShapeDtypeStruct((share, long), BF)] * (mp_size - 1),
        [SMEM] + [VMEM] * 11,
        [pltpu.VMEM((keep, width), F32), pltpu.VMEM((keep, long), F32)],
    )(
        jnp.stack([flag, mp_at]),
        total,
        norm,
        middle,
        rows,
        rows_squares,
        own_out,
        other_out,
        own_lvalue,
        other_lvalue,
        own_lout,
        other_lout,
    )
    scored, kept, kept_norm = outs[:3]
    every_scored = lax.all_gather(scored, ("segment", "dp"), axis=0, tiled=False)
    got = lax.optimization_barrier(
        tuple(flip(peer, "mp", mask) for mask, peer in enumerate(outs[3:], 1))
    )
    direct = dp_size <= 8 and block % SIDE == 0
    pieces = call(
        functools.partial(value_kernel, learner_width, block, mp_size - 1),
        [jax.ShapeDtypeStruct((share, inner + block + SIDE), BF)] * dp_size
        if direct
        else [jax.ShapeDtypeStruct((share, long), BF)],
        [SMEM] + [VMEM] * (mp_size + 1),
        [pltpu.VMEM((share, inner), BF)],
    )(jnp.stack([dp_at]), kept, kept_norm, *got)

    gram_half = jnp.sum(gram_parts.astype(F32), axis=0).astype(BF)
    gram_other = flip(gram_half, "segment", 1)
    gram = jnp.where(
        first,
        jnp.concatenate([gram_half, gram_other], axis=0),
        jnp.concatenate([gram_other, gram_half], axis=0),
    )

    goals = every_row[:, :, width].astype(jnp.int32).reshape(2, dp_size, keep)
    hits = goals[:, :, :, None] == jnp.arange(1, dp_size + 1)
    counts = jnp.sum(hits.astype(F32), axis=(1, 2), keepdims=True)
    parts = 1.0 / jnp.maximum(jnp.sum(jnp.where(hits, counts, 0.0), axis=3), 1.0)
    column = dp_at * block

    def spread(piece):
        whole = jnp.zeros((keep, piece.shape[1]), BF)
        for mask in range(mp_size):
            got = flip(piece, "mp", mask) if mask else piece
            whole = lax.dynamic_update_slice(whole, got, ((mp_at ^ mask) * share, 0))
        return whole

    def add(grads, pieces, places):
        pieces = jnp.concatenate(pieces, axis=0)
        tokens = jnp.concatenate([pieces, flip(pieces, "segment", 1)], axis=0)
        x, share_count = [], []
        for segment in (at, 1 - at):
            for place in places:
                row = lax.dynamic_index_in_dim(every_row, segment * dp_size + place, 0, False)
                score = lax.dynamic_index_in_dim(every_scored, segment * dp_size + place, 0, False)
                x.append(jnp.where(first, row[:, :width], score))
                share_count.append(lax.dynamic_slice(parts, (segment, place, 0), (1, 1, keep)))
        x = jnp.concatenate(x, axis=0).astype(F32)
        share_count = jnp.concatenate([part.reshape(keep, 1) for part in share_count], axis=0)
        v = tokens[:, :inner]
        xo = tokens[:, inner : inner + block].astype(F32)
        inv = unpack(tokens[:, inner + block :], 0)
        slopes = ((x + matmul(v, own_lout)) * share_count).astype(BF)
        normed = (x * inv).astype(BF)
        back = ((xo + matmul(v, gram)) * share_count).astype(BF)
        v_block = lax.dynamic_slice_in_dim(v, column, block, 1)
        return (grads[0] + matmul_tn(back, normed), grads[1] + matmul_tn(v_block, slopes))

    if direct:
        moved = [flip(pieces[away], "dp", away) for away in range(1, dp_size)]
        rest = jnp.concatenate(lax.optimization_barrier(tuple(moved)), axis=1)
        groups = []
        for piece in (pieces[0], rest):
            for mask in range(mp_size):
                near = flip(piece, "mp", mask) if mask else piece
                groups += [near, flip(near, "segment", 1)]
        tokens = 2 * dp_size * keep
        grads = call(
            functools.partial(gradient_kernel, share, mp_size, dp_size),
            [jax.ShapeDtypeStruct((block, width), F32)] * 2,
            [SMEM] + [HBM] * (len(groups) + 2) + [VMEM] * 3,
            [
                pltpu.VMEM((tokens, inner + block + SIDE), BF),
                pltpu.VMEM((tokens, width), BF),
                pltpu.VMEM((tokens, width), BF),
                pltpu.VMEM((tokens, width), BF),
                pltpu.VMEM((tokens, block), BF),
                pltpu.SemaphoreType.DMA((tokens // share,)),
                pltpu.SemaphoreType.DMA,
            ],
        )(
            jnp.stack([flag, dp_at, mp_at]),
            *groups,
            every_row.reshape(tokens, width + SIDE),
            every_scored.reshape(tokens, width),
            parts.reshape(tokens, 1),
            own_lout,
            gram,
        )
    else:
        ring = [(source, (source + 1) % dp_size) for source in range(dp_size)]

        def turn(step, carry):
            grads, full = carry
            cross = lax.dynamic_slice_in_dim(full, inner + column, block, 1)
            piece = jnp.concatenate([full[:, :inner], cross, full[:, 2 * inner :]], axis=1)
            grads = add(grads, [spread(piece)], [(dp_at - step) % dp_size])
            return grads, lax.ppermute(full, "dp", ring)

        grads = (jnp.zeros((block, width), F32), jnp.zeros((block, width), F32))
        grads, _ = lax.fori_loop(0, dp_size, turn, (grads, pieces[0]))
    return (grads[0][None], grads[1][None])


def solution(mesh):
    placed = (
        P(("segment", "dp"), "mp"),
        P("segment", "mp", None),
        P("segment", None, "mp"),
        P("segment", "mp", None),
        P("segment", None, "mp"),
        P(("segment", "dp"), None),
        P(("segment", "dp"), None),
        P(("segment", "dp")),
    )
    return jax.shard_map(
        on_device,
        mesh=mesh,
        in_specs=placed,
        out_specs=(P("segment", "dp", "mp"), P("segment", "dp", "mp")),
        check_vma=False,
    )
```

```python
import functools

import jax
import jax.numpy as jnp
from jax import lax
from jax.experimental import pallas as pl
from jax.experimental.pallas import tpu as pltpu
from jax.sharding import PartitionSpec as P

EPSILON = 1e-05
BF = jnp.bfloat16
F32 = jnp.float32
SIDE = 128


def flip(value, axis, mask):
    pairs = [(source, source ^ mask) for source in range(lax.axis_size(axis))]
    return lax.ppermute(value, axis, pairs)


def matmul(left, right):
    return jnp.dot(left, right, preferred_element_type=F32)


def matmul_nt(left, right):
    return lax.dot_general(left, right, (((1,), (1,)), ((), ())), preferred_element_type=F32)


def matmul_tn(left, right):
    return lax.dot_general(left, right, (((0,), (0,)), ((), ())), preferred_element_type=F32)


def unpack(side, place):
    wide = side[:, 3 * place : 3 * place + 3].astype(F32)
    return wide[:, 0:1] + wide[:, 1:2] + wide[:, 2:3]


VMEM = pl.BlockSpec(memory_space=pltpu.VMEM)
SMEM = pl.BlockSpec(memory_space=pltpu.SMEM)
HBM = pl.BlockSpec(memory_space=pltpu.HBM)


def call(body, outs, in_specs, scratch=(), mebibytes=4, out_specs=None):
    return pl.pallas_call(
        body,
        out_shape=outs,
        in_specs=in_specs,
        out_specs=out_specs or [VMEM] * len(outs),
        scratch_shapes=list(scratch),
        compiler_params=pltpu.CompilerParams(vmem_limit_bytes=mebibytes << 20),
    )


def fetch(take_left, left, right, target, sem):
    @pl.when(take_left)
    def _():
        pltpu.make_async_copy(left, target, sem).start()

    @pl.when(jnp.logical_not(take_left))
    def _():
        pltpu.make_async_copy(right, target, sem).start()


def start_copy(source, target, sem):
    copy = pltpu.make_async_copy(source, target, sem)
    copy.start()
    return copy


def side_of(column):
    lane = lax.broadcasted_iota(jnp.int32, (column.shape[0], SIDE), 1)
    high = column.astype(BF).astype(F32)
    middle = (column - high).astype(BF).astype(F32)
    low = column - high - middle
    zero = jnp.zeros(lane.shape, F32)
    picked = jnp.where(lane == 0, high, jnp.where(lane == 1, middle, jnp.where(lane == 2, low, zero)))
    return picked.astype(BF)


def from_side(side):
    return jnp.sum(side.astype(F32), axis=1, keepdims=True)


def emit(part, norm, sents, gram=None):
    half, width = sents[0].shape[0], part.shape[1]
    for place, sent in enumerate(sents):
        start = place * half
        sent[:, :width] = part[start : start + half, :].astype(BF)
        sent[:, width : width + SIDE] = side_of(norm[start : start + half, :])
        if gram is not None:
            for rows, columns in gram_blocks(gram, place, half, width):
                sent[:, columns] = gram[rows, :].astype(BF)


def gram_blocks(gram, place, half, width):
    count, block = gram.shape[0] // 2 // half, gram.shape[1]
    for index in range(count):
        row = (place * count + index) * half
        column = width + SIDE + index * block
        yield slice(row, row + half), slice(column, column + block)


def absorb(part, norm, gots, gram=None, gram_sum=None):
    half, width = gots[0].shape[0], part.shape[1]
    parts, norms = [], []
    for place, got in enumerate(gots):
        start = place * half
        parts.append(part[start : start + half, :] + got[:, :width].astype(F32))
        side = got[:, width : width + SIDE]
        norms.append(norm[start : start + half, :] + from_side(side))
        if gram is not None:
            for rows, columns in gram_blocks(gram, place, half, width):
                summed = gram[rows, :] + got[:, columns].astype(F32)
                gram_sum[rows, :] = summed.astype(gram_sum.dtype)
    return jnp.concatenate(parts, axis=0), jnp.concatenate(norms, axis=0)


def start_kernel(with_gram, where, rows, value_a, value_b, *refs):
    gram_a, gram_b = refs[:2] if with_gram else (None, None)
    refs = refs[2:] if with_gram else refs
    part, norm, top, low = refs[:4]
    gram, (weight, sem) = refs[4] if with_gram else None, refs[-2:]
    fetch(where[0] == 1, value_a, value_b, weight, sem)
    row = rows[...]
    norm[...] = square_sum(row)
    if with_gram:
        gram[...] = gram_a[...] + gram_b[...].astype(F32)
    pltpu.make_async_copy(value_a, weight, sem).wait()
    part[...] = matmul(row, weight[...])
    emit(part, norm, (top, low), gram)


def between_kernel(with_gram, part_in, norm_in, got_top, got_low, *refs):
    gram_in, refs = (refs[0], refs[1:]) if with_gram else (None, refs)
    part, norm, top, low = refs[:4]
    gram = refs[4] if with_gram else None
    part[...], norm[...] = absorb(part_in, norm_in, (got_top, got_low), gram_in, gram)
    emit(part, norm, (top, low), gram)


def section_kernel(features, with_gram, where, *refs):
    part_in, norm_in, got_top, got_low, rows, out_a, out_b, value_a, value_b = refs[:9]
    gram_in, refs = (refs[9], refs[10:]) if with_gram else (None, refs[9:])
    middle, part, norm, top, low = refs[:5]
    gram, (out, value, sems) = refs[5] if with_gram else None, refs[-3:]
    first = where[0] == 1
    fetch(first, out_a, out_b, out, sems.at[0])
    fetch(first, value_b, value_a, value, sems.at[1])
    total, squares = absorb(part_in, norm_in, (got_top, got_low), gram_in, gram)
    values = (total * lax.rsqrt(squares / features + EPSILON)).astype(BF)
    pltpu.make_async_copy(out_a, out, sems.at[0]).wait()
    hidden = (rows[...].astype(F32) + matmul(values, out[...])).astype(BF)
    middle[...] = hidden
    norm[...] = square_sum(hidden)
    pltpu.make_async_copy(value_a, value, sems.at[1]).wait()
    part[...] = matmul(hidden, value[...])
    emit(part, norm, (top, low))


def learn_kernel(where, rows, value_a, value_b, lout_a, lout_b, part, value, lout, sems):
    first = where[0] == 1
    fetch(first, value_a, value_b, value, sems.at[0])
    fetch(first, lout_a, lout_b, lout, sems.at[1])
    inner = value.shape[1]
    pltpu.make_async_copy(value_a, value, sems.at[0]).wait()
    part[:, :inner] = matmul(rows[...], value[...])
    pltpu.make_async_copy(lout_a, lout, sems.at[1]).wait()
    part[:, inner:] = matmul_nt(rows[...], lout[...])


def score_kernel(features, where, *refs):
    part_in, norm_in, got_top, got_low, middle, rows_squares, out_a, out_b = refs[:8]
    scored, norm, out, sem = refs[8:]
    fetch(where[0] == 1, out_b, out_a, out, sem)
    total, squares = absorb(part_in, norm_in, (got_top, got_low))
    values = (total * lax.rsqrt(squares / features + EPSILON)).astype(BF)
    pltpu.make_async_copy(out_a, out, sem).wait()
    score = (middle[...].astype(F32) + matmul(values, out[...])).astype(BF)
    scored[...] = score
    norm[...] = rows_squares[...] + square_sum(score)


def share_kernel(share, where, scored, norm, given, value_a, value_b, lout_a, lout_b, *refs):
    kept, kept_norm = refs[:2]
    peers, (value, lout, part, sent, sems) = refs[2:-5], refs[-5:]
    first, at = where[0] == 1, where[1]
    fetch(first, value_b, value_a, value, sems.at[0])
    fetch(first, lout_b, lout_a, lout, sems.at[1])
    inner = value.shape[1]
    score = scored[...]
    sent[:, 2 * inner :] = side_of(norm[...])
    pltpu.make_async_copy(value_a, value, sems.at[0]).wait()
    part[:, :inner] = given[:, :inner] + matmul(score, value[...])
    sent[:, :inner] = part[:, :inner].astype(BF)
    pltpu.make_async_copy(lout_a, lout, sems.at[1]).wait()
    part[:, inner:] = given[:, inner:] + matmul_nt(score, lout[...])
    sent[:, inner : 2 * inner] = part[:, inner:].astype(BF)
    copies = []
    for place, peer in enumerate(peers):
        start = pl.multiple_of((at ^ (place + 1)) * share, share)
        copies.append(start_copy(sent.at[pl.ds(start, share), :], peer, sems.at[2 + place]))
    mine = pl.ds(pl.multiple_of(at * share, share), share)
    kept[...] = part[mine, :]
    kept_norm[...] = norm[mine, :]
    for copy in copies:
        copy.wait()


def value_kernel(features, block, count, where, kept, norm, *refs):
    got, pieces, crossed = refs[:count], refs[count:-1], refs[-1]
    total, squares = kept[...], norm[...]
    inner = total.shape[1] // 2
    for one in got:
        total = total + one[:, : 2 * inner].astype(F32)
        squares = squares + from_side(one[:, 2 * inner :])
    inverse = lax.rsqrt(squares / features + EPSILON)
    values = (total[:, :inner] * inverse).astype(BF)
    side = side_of(inverse)
    crossed[...] = total[:, inner:].astype(BF)
    for away, piece in enumerate(pieces):
        if len(pieces) == 1:
            cross = crossed[...]
        else:
            cross = crossed[:, pl.ds(pl.multiple_of((where[0] ^ away) * block, block), block)]
        reach = inner + cross.shape[1]
        piece[:, :inner] = values
        piece[:, inner:reach] = cross
        piece[:, reach:] = side


def gradient_kernel(share, peers, aways, spots, dp_size, where, *refs):
    groups = 1 + max(group for group, _ in spots)
    count = 2 * peers * groups
    sources, refs = refs[:count], refs[count:]
    inputs, dense = refs[:2], refs[2:-12]
    parts, grad_value, grad_out, tokens, x, slopes, normed, back, share_count = refs[-12:-3]
    lout, gram, sems = refs[-3:]
    given = dense[2:]
    first, dp_at, mp_at = where[0] == 1, where[1], where[2]
    keep = share * peers
    width, inner, block = x.shape[1], lout.shape[0], gram.shape[1]
    piece = inner + block + SIDE
    total = tokens.shape[0]
    copies = []

    def begin(source, target):
        copies.append(start_copy(source, target, sems.at[len(copies)]))

    begin(dense[0], lout)
    begin(dense[1], gram)
    for array, target in zip(given, (grad_value, grad_out)):
        begin(array, target)
    ready = []
    for number, (away, (group, place)) in enumerate(zip(aways, spots)):
        for side in range(2):
            segment = jnp.where(first, side, 1 - side)
            start = (2 * number + side) * keep
            row = pl.multiple_of((segment * dp_size + (dp_at ^ away)) * keep, keep)
            share_count[start : start + keep, :] = parts[pl.ds(row, keep), :]
            target = x.at[pl.ds(start, keep), :]
            if away == 0:
                begin(inputs[side], target)
            else:
                here, sem = pl.ds(row, keep), sems.at[len(copies)]
                fetch(first, inputs[0].at[here, pl.ds(0, width)], inputs[1].at[here, :], target, sem)
                copies.append(pltpu.make_async_copy(inputs[1].at[here, :], target, sem))
            for mask in range(peers):
                source = sources[2 * (group * peers + mask) + side]
                at = pl.multiple_of(start + (mp_at ^ mask) * share, share)
                begin(
                    source.at[:, pl.ds(place * piece, piece)],
                    tokens.at[pl.ds(at, share), :],
                )
        ready.append(len(copies))
    fixed = 2 + len(given)
    for copy in copies[:2]:
        copy.wait()
    done = fixed
    for number, until in enumerate(ready):
        for copy in copies[done:until]:
            copy.wait()
        done = until
        here = pl.ds(2 * keep * number, 2 * keep)
        wide = x[here, :].astype(F32)
        values = tokens[here, :inner]
        inverse = from_side(tokens[here, inner + block :])
        portion = share_count[here, :]
        slopes[here, :] = ((wide + matmul(values, lout[...])) * portion).astype(BF)
        normed[here, :] = (wide * inverse).astype(BF)
        crossed = tokens[here, inner : inner + block].astype(F32)
        back[here, :] = ((crossed + matmul(values, gram[...])) * portion).astype(BF)
    for copy in copies[2:fixed]:
        copy.wait()
    column = pl.ds(pl.multiple_of(dp_at * block, block), block)
    value_sum = matmul_tn(back[...], normed[...])
    out_sum = matmul_tn(tokens[:, column], slopes[...])
    if given:
        value_sum = value_sum + grad_value[...]
        out_sum = out_sum + grad_out[...]
    grad_value[...] = value_sum
    grad_out[...] = out_sum


def square_sum(value):
    wide = value.astype(F32)
    return jnp.sum(wide * wide, axis=1, keepdims=True)


def exchange(first, second, first_mask, second_mask):
    first, second = lax.optimization_barrier((first, second))
    return lax.optimization_barrier(
        (flip(first, "mp", first_mask), flip(second, "mp", second_mask))
    )


def on_device(
    candidates,
    scorer_value,
    scorer_out,
    learner_value,
    learner_out,
    keep_index,
    keep_dest,
    keep_count,
):
    first = lax.axis_index("segment") == 0
    dp_at = lax.axis_index("dp")
    mp_at = lax.axis_index("mp")
    dp_size = lax.axis_size("dp")
    mp_size = lax.axis_size("mp")
    keep = keep_index.shape[1]
    width = candidates.shape[1]
    scorer_width = width * mp_size
    learner_width = 2 * scorer_width
    inner = learner_value.shape[2]
    block = inner // dp_size
    share = keep // mp_size

    own_value, own_out = scorer_value[0], scorer_out[0]
    own_lvalue, own_lout = learner_value[0], learner_out[0]
    other_value = flip(own_value, "segment", 1)

    is_live = jnp.arange(keep) < keep_count[0]
    pick = (keep_index[0][:, None] == jnp.arange(candidates.shape[0])[None, :]) & is_live[:, None]
    rows = matmul(pick.astype(BF), candidates).astype(BF)
    goal = jnp.where(is_live, keep_dest[0] + 1, 0).astype(F32)[:, None]
    every_row = lax.all_gather(
        jnp.concatenate([rows, jnp.broadcast_to(goal, (keep, SIDE)).astype(BF)], axis=1),
        ("segment", "dp"),
        axis=0,
        tiled=False,
    )

    gram = matmul_nt(own_lout, lax.dynamic_slice_in_dim(own_lout, dp_at * block, block, 0))
    half = inner // 2
    at = lax.axis_index("segment")
    kept_half = lax.dynamic_slice_in_dim(gram, at * half, half, 0)
    sent_half = lax.dynamic_slice_in_dim(gram, (1 - at) * half, half, 0)
    got_half = flip(sent_half.astype(BF), "segment", 1)

    direct = dp_size <= 8 and block % SIDE == 0
    flag = first.astype(jnp.int32)
    half_rows = keep // 2
    sums = [jax.ShapeDtypeStruct((keep, inner), F32), jax.ShapeDtypeStruct((keep, 1), F32)]
    state = sums + [jax.ShapeDtypeStruct((half_rows, inner + SIDE), BF)] * 2
    wide_state = state
    if direct:
        extra = half * block // keep
        wide_state = sums + [jax.ShapeDtypeStruct((half_rows, inner + SIDE + extra), BF)] * 2
        wide_state.append(jax.ShapeDtypeStruct((half, block), F32))
    hidden_type = jax.ShapeDtypeStruct((keep, width), BF)
    where = jnp.stack([flag, mp_at])
    weight = pltpu.VMEM(own_value.shape, BF)

    def placed(*arrays):
        return [pltpu.with_memory_space_constraint(array, pltpu.HBM) for array in arrays]

    def halves(outs):
        return outs[0], outs[1], outs[2:4], list(outs[4:])

    outs = call(
        functools.partial(start_kernel, direct),
        wide_state,
        [SMEM, VMEM, HBM, HBM] + [VMEM] * (2 * direct),
        [weight, pltpu.SemaphoreType.DMA],
        mebibytes=12,
    )(where, rows, *placed(own_value, other_value), *((kept_half, got_half) if direct else ()))
    part, rows_squares, sents, gram_sum = halves(outs)
    own_out, own_lvalue, own_lout, sents = lax.optimization_barrier(
        (own_out, own_lvalue, own_lout, sents)
    )
    other_out = flip(own_out, "segment", 1)
    other_lvalue = flip(own_lvalue, "segment", 1)
    other_lout = flip(own_lout, "segment", 1)
    got = exchange(*sents, 1, 2)
    outs = call(
        functools.partial(between_kernel, direct), wide_state, [VMEM] * (4 + direct), mebibytes=8
    )(part, rows_squares, *got, *gram_sum)
    part, norm, sents, gram_sum = halves(outs)
    got = exchange(*sents, 2, 1)
    outs = call(
        functools.partial(section_kernel, scorer_width, direct),
        [hidden_type] + state + [jax.ShapeDtypeStruct((half, block), BF)] * direct,
        [SMEM] + [VMEM] * 5 + [HBM] * 4 + [VMEM] * direct,
        [weight, weight, pltpu.SemaphoreType.DMA((2,))],
        mebibytes=12,
    )(where, part, norm, *got, rows, *placed(own_out, other_out, own_value, other_value), *gram_sum)
    middle, outs = outs[0], outs[1:]
    part, norm, sents, gram_sum = halves(outs)
    learner_weights = placed(own_lvalue, other_lvalue, own_lout, other_lout)
    given = call(
        learn_kernel,
        [jax.ShapeDtypeStruct((keep, 2 * inner), F32)],
        [SMEM, VMEM] + [HBM] * 4,
        [weight, weight, pltpu.SemaphoreType.DMA((2,))],
        mebibytes=10,
    )(where, rows, *learner_weights)[0]
    got = exchange(*sents, 1, 2)
    outs = call(functools.partial(between_kernel, False), state, [VMEM] * 4)(part, norm, *got)
    part, norm, sents, _ = halves(outs)
    sents, given = lax.optimization_barrier((sents, given))
    got = exchange(*sents, 2, 1)
    part, goals = lax.optimization_barrier((part, every_row[:, :, width]))

    long = 2 * inner + SIDE
    scored, norm = call(
        functools.partial(score_kernel, scorer_width),
        [hidden_type, sums[1]],
        [SMEM] + [VMEM] * 6 + [HBM] * 2,
        [weight, pltpu.SemaphoreType.DMA],
        mebibytes=8,
    )(where, part, norm, *got, middle, rows_squares, *placed(own_out, other_out))
    every_scored = lax.all_gather(scored, ("segment", "dp"), axis=0, tiled=False)
    outs = call(
        functools.partial(share_kernel, share),
        [
            jax.ShapeDtypeStruct((share, 2 * inner), F32),
            jax.ShapeDtypeStruct((share, 1), F32),
        ]
        + [pltpu.HBM((share, long), BF)] * (mp_size - 1),
        [SMEM] + [VMEM] * 3 + [HBM] * 4,
        [
            weight,
            weight,
            pltpu.VMEM((keep, 2 * inner), F32),
            pltpu.VMEM((keep, long), BF),
            pltpu.SemaphoreType.DMA((mp_size + 1,)),
        ],
        mebibytes=12,
        out_specs=[VMEM] * 2 + [HBM] * (mp_size - 1),
    )(where, scored, norm, given, *learner_weights)
    kept, kept_norm = outs[:2]
    got = lax.optimization_barrier(
        tuple(flip(peer, "mp", mask) for mask, peer in enumerate(outs[2:], 1))
    )
    pieces = call(
        functools.partial(value_kernel, learner_width, block, mp_size - 1),
        [jax.ShapeDtypeStruct((share, inner + block + SIDE), BF)] * dp_size
        if direct
        else [jax.ShapeDtypeStruct((share, long), BF)],
        [SMEM] + [VMEM] * (mp_size + 1),
        [pltpu.VMEM((share, inner), BF)],
    )(jnp.stack([dp_at]), kept, kept_norm, *got)

    if direct:
        gram_half = gram_sum[0]
    else:
        gram_half = lax.psum(kept_half + got_half.astype(F32), "mp").astype(BF)
    gram_other = flip(gram_half, "segment", 1)
    gram = jnp.where(
        first,
        jnp.concatenate([gram_half, gram_other], axis=0),
        jnp.concatenate([gram_other, gram_half], axis=0),
    )

    goals = goals.astype(jnp.int32).reshape(2, dp_size, keep)
    hits = goals[:, :, :, None] == jnp.arange(1, dp_size + 1)
    counts = jnp.sum(hits.astype(F32), axis=(1, 2), keepdims=True)
    parts = 1.0 / jnp.maximum(jnp.sum(jnp.where(hits, counts, 0.0), axis=3), 1.0)
    column = dp_at * block

    def spread(piece):
        whole = jnp.zeros((keep, piece.shape[1]), BF)
        for mask in range(mp_size):
            got = flip(piece, "mp", mask) if mask else piece
            whole = lax.dynamic_update_slice(whole, got, ((mp_at ^ mask) * share, 0))
        return whole

    def add(grads, pieces, places):
        pieces = jnp.concatenate(pieces, axis=0)
        tokens = jnp.concatenate([pieces, flip(pieces, "segment", 1)], axis=0)
        x, share_count = [], []
        for segment in (at, 1 - at):
            for place in places:
                row = lax.dynamic_index_in_dim(every_row, segment * dp_size + place, 0, False)
                score = lax.dynamic_index_in_dim(every_scored, segment * dp_size + place, 0, False)
                x.append(jnp.where(first, row[:, :width], score))
                share_count.append(lax.dynamic_slice(parts, (segment, place, 0), (1, 1, keep)))
        x = jnp.concatenate(x, axis=0).astype(F32)
        share_count = jnp.concatenate([part.reshape(keep, 1) for part in share_count], axis=0)
        v = tokens[:, :inner]
        xo = tokens[:, inner : inner + block].astype(F32)
        inv = unpack(tokens[:, inner + block :], 0)
        slopes = ((x + matmul(v, own_lout)) * share_count).astype(BF)
        normed = (x * inv).astype(BF)
        back = ((xo + matmul(v, gram)) * share_count).astype(BF)
        v_block = lax.dynamic_slice_in_dim(v, column, block, 1)
        return (grads[0] + matmul_tn(back, normed), grads[1] + matmul_tn(v_block, slopes))

    if direct:
        moved = [flip(pieces[away], "dp", away) for away in range(1, dp_size)]
        stacks = [[pieces[0]] + moved[:1], moved[1:]]

        def all_shares(stack):
            stack = jnp.concatenate(stack, axis=1) if len(stack) > 1 else stack[0]
            return [stack] + [flip(stack, "mp", mask) for mask in range(1, mp_size)]

        def both_cores(nears):
            return [array for near in nears for array in (near, flip(near, "segment", 1))]

        swap = flip(jnp.where(first, scored, rows), "segment", 1)
        near_x = jnp.where(first, rows, scored)
        whole = parts.reshape(2 * dp_size * keep, 1)
        where = jnp.stack([flag, dp_at, mp_at])

        def gradients(aways, spots, groups, inputs, given, mebibytes):
            tokens = 2 * len(aways) * keep
            dense = [own_lout, gram, *given]
            return call(
                functools.partial(gradient_kernel, share, mp_size, aways, spots, dp_size),
                [jax.ShapeDtypeStruct((block, width), F32)] * 2,
                [SMEM] + [HBM] * (len(groups) + 2 + len(dense)) + [VMEM],
                [
                    pltpu.VMEM((tokens, inner + block + SIDE), BF),
                    pltpu.VMEM((tokens, width), BF),
                    pltpu.VMEM((tokens, width), BF),
                    pltpu.VMEM((tokens, width), BF),
                    pltpu.VMEM((tokens, block), BF),
                    pltpu.VMEM((tokens, 1), F32),
                    pltpu.VMEM(own_lout.shape, BF),
                    pltpu.VMEM(gram.shape, BF),
                    pltpu.SemaphoreType.DMA((2 * len(aways) * (mp_size + 1) + len(dense),)),
                ],
                mebibytes=mebibytes,
            )(where, *placed(*groups, *inputs, *dense), whole)

        early = all_shares(stacks[0])
        early[1:] = lax.optimization_barrier(early[1:])
        groups = both_cores(early)
        grads = gradients((0,), ((0, 0),), groups, (near_x, swap), (), 14)
        if dp_size > 1:
            spots = ((0, 1),)
            if dp_size > 2:
                *stack, _ = lax.optimization_barrier((*stacks[1], early[1:]))
                late = all_shares(stack)
                last, grads = lax.optimization_barrier((late[-1], grads))
                groups = groups + both_cores(late[:-1] + [last])
                spots += tuple((1, place) for place in range(dp_size - 2))
            tokens = 2 * dp_size * keep
            inputs = (
                every_row.reshape(tokens, width + SIDE),
                every_scored.reshape(tokens, width),
            )
            grads = gradients(tuple(range(1, dp_size)), spots, groups, inputs, grads, 22)
    else:
        ring = [(source, (source + 1) % dp_size) for source in range(dp_size)]

        def turn(step, carry):
            grads, full = carry
            cross = lax.dynamic_slice_in_dim(full, inner + column, block, 1)
            piece = jnp.concatenate([full[:, :inner], cross, full[:, 2 * inner :]], axis=1)
            grads = add(grads, [spread(piece)], [(dp_at - step) % dp_size])
            return grads, lax.ppermute(full, "dp", ring)

        grads = (jnp.zeros((block, width), F32), jnp.zeros((block, width), F32))
        grads, _ = lax.fori_loop(0, dp_size, turn, (grads, pieces[0]))
    return (grads[0][None], grads[1][None])


def solution(mesh):
    placed = (
        P(("segment", "dp"), "mp"),
        P("segment", "mp", None),
        P("segment", None, "mp"),
        P("segment", "mp", None),
        P("segment", None, "mp"),
        P(("segment", "dp"), None),
        P(("segment", "dp"), None),
        P(("segment", "dp")),
    )
    return jax.shard_map(
        on_device,
        mesh=mesh,
        in_specs=placed,
        out_specs=(P("segment", "dp", "mp"), P("segment", "dp", "mp")),
        check_vma=False,
    )
```

```python
import functools

import jax
import jax.numpy as jnp
from jax import lax
from jax.experimental import pallas as pl
from jax.experimental.pallas import tpu as pltpu
from jax.sharding import PartitionSpec as P

EPSILON = 1e-05
BF = jnp.bfloat16
F32 = jnp.float32
SIDE = 128


def flip(value, axis, mask):
    pairs = [(source, source ^ mask) for source in range(lax.axis_size(axis))]
    return lax.ppermute(value, axis, pairs)


def matmul(left, right):
    return jnp.dot(left, right, preferred_element_type=F32)


def matmul_nt(left, right):
    return lax.dot_general(left, right, (((1,), (1,)), ((), ())), preferred_element_type=F32)


def matmul_tn(left, right):
    return lax.dot_general(left, right, (((0,), (0,)), ((), ())), preferred_element_type=F32)


def unpack(side, place):
    wide = side[:, 3 * place : 3 * place + 3].astype(F32)
    return wide[:, 0:1] + wide[:, 1:2] + wide[:, 2:3]


VMEM = pl.BlockSpec(memory_space=pltpu.VMEM)
SMEM = pl.BlockSpec(memory_space=pltpu.SMEM)
HBM = pl.BlockSpec(memory_space=pltpu.HBM)


def call(body, outs, in_specs, scratch=(), mebibytes=4, out_specs=None, cost=None):
    return pl.pallas_call(
        body,
        out_shape=outs,
        in_specs=in_specs,
        out_specs=out_specs or [VMEM] * len(outs),
        scratch_shapes=list(scratch),
        compiler_params=pltpu.CompilerParams(vmem_limit_bytes=mebibytes << 20),
        cost_estimate=cost,
    )


def fetch(take_left, left, right, target, sem):
    @pl.when(take_left)
    def _():
        pltpu.make_async_copy(left, target, sem).start()

    @pl.when(jnp.logical_not(take_left))
    def _():
        pltpu.make_async_copy(right, target, sem).start()


def start_copy(source, target, sem):
    copy = pltpu.make_async_copy(source, target, sem)
    copy.start()
    return copy


def side_of(*columns):
    lane = lax.broadcasted_iota(jnp.int32, (columns[0].shape[0], SIDE), 1)
    picked = jnp.zeros(lane.shape, F32)
    for place, column in enumerate(columns):
        high = column.astype(BF).astype(F32)
        middle = (column - high).astype(BF).astype(F32)
        for part, piece in enumerate((high, middle, column - high - middle)):
            picked = jnp.where(lane == 3 * place + part, piece, picked)
    return picked.astype(BF)


def from_side(side, place=0):
    lane = lax.broadcasted_iota(jnp.int32, side.shape, 1)
    own = (lane >= 3 * place) & (lane < 3 * place + 3)
    return jnp.sum(jnp.where(own, side.astype(F32), 0.0), axis=1, keepdims=True)


def emit(part, norm, sents, gram=None):
    half, width = sents[0].shape[0], part.shape[1]
    for place, sent in enumerate(sents):
        start = place * half
        sent[:, :width] = part[start : start + half, :].astype(BF)
        sent[:, width : width + SIDE] = side_of(norm[start : start + half, :])
        if gram is not None:
            for rows, columns in gram_blocks(gram, place, half, width):
                sent[:, columns] = gram[rows, :].astype(BF)


def gram_blocks(gram, place, half, width):
    count, block = gram.shape[0] // 2 // half, gram.shape[1]
    for index in range(count):
        row = (place * count + index) * half
        column = width + SIDE + index * block
        yield slice(row, row + half), slice(column, column + block)


def absorb(part, norm, gots, gram=None, gram_sum=None):
    half, width = gots[0].shape[0], part.shape[1]
    parts, norms = [], []
    for place, got in enumerate(gots):
        start = place * half
        parts.append(part[start : start + half, :] + got[:, :width].astype(F32))
        side = got[:, width : width + SIDE]
        norms.append(norm[start : start + half, :] + from_side(side))
        if gram is not None:
            for rows, columns in gram_blocks(gram, place, half, width):
                summed = gram[rows, :] + got[:, columns].astype(F32)
                gram_sum[rows, :] = summed.astype(gram_sum.dtype)
    return jnp.concatenate(parts, axis=0), jnp.concatenate(norms, axis=0)


def repeat_kernel(array, repeated, sems):
    rows = array.shape[0]
    copies = [
        start_copy(array, repeated.at[pl.ds(place * rows, rows), :], sems.at[place])
        for place in range(repeated.shape[0] // rows)
    ]
    for copy in copies:
        copy.wait()


def start_kernel(with_gram, where, rows, value_a, value_b, *refs):
    gram_a, gram_b = refs[:2] if with_gram else (None, None)
    refs = refs[2:] if with_gram else refs
    part, norm, top, low = refs[:4]
    gram, (weight, sem) = refs[4] if with_gram else None, refs[-2:]
    fetch(where[0] == 1, value_a, value_b, weight, sem)
    row = rows[...]
    norm[...] = square_sum(row)
    if with_gram:
        gram[...] = gram_a[...] + gram_b[...].astype(F32)
    pltpu.make_async_copy(value_a, weight, sem).wait()
    part[...] = matmul(row, weight[...])
    emit(part, norm, (top, low), gram)


def between_kernel(with_gram, part_in, norm_in, got_top, got_low, *refs):
    gram_in, refs = (refs[0], refs[1:]) if with_gram else (None, refs)
    part, norm, top, low = refs[:4]
    gram = refs[4] if with_gram else None
    part[...], norm[...] = absorb(part_in, norm_in, (got_top, got_low), gram_in, gram)
    emit(part, norm, (top, low), gram)


def section_kernel(features, with_gram, where, *refs):
    part_in, norm_in, got_top, got_low, rows, out_a, out_b, value_a, value_b = refs[:9]
    gram_in, refs = (refs[9], refs[10:]) if with_gram else (None, refs[9:])
    middle, part, norm, top, low = refs[:5]
    gram, (out, value, sems) = refs[5] if with_gram else None, refs[-3:]
    first = where[0] == 1
    fetch(first, out_a, out_b, out, sems.at[0])
    fetch(first, value_b, value_a, value, sems.at[1])
    total, squares = absorb(part_in, norm_in, (got_top, got_low), gram_in, gram)
    values = (total * lax.rsqrt(squares / features + EPSILON)).astype(BF)
    pltpu.make_async_copy(out_a, out, sems.at[0]).wait()
    hidden = (rows[...].astype(F32) + matmul(values, out[...])).astype(BF)
    middle[...] = hidden
    norm[...] = square_sum(hidden)
    pltpu.make_async_copy(value_a, value, sems.at[1]).wait()
    part[...] = matmul(hidden, value[...])
    emit(part, norm, (top, low))


def learn_kernel(where, rows, value_a, value_b, lout_a, lout_b, part, value, lout, sems):
    first = where[0] == 1
    fetch(first, value_a, value_b, value, sems.at[0])
    fetch(first, lout_a, lout_b, lout, sems.at[1])
    inner = value.shape[1]
    pltpu.make_async_copy(value_a, value, sems.at[0]).wait()
    part[:, :inner] = matmul(rows[...], value[...])
    pltpu.make_async_copy(lout_a, lout, sems.at[1]).wait()
    part[:, inner:] = matmul_nt(rows[...], lout[...])


def score_kernel(features, where, *refs):
    part_in, norm_in, got_top, got_low, middle, rows_squares, out_a, out_b = refs[:8]
    scored, norm, repeated, out, sems = refs[8:]
    fetch(where[0] == 1, out_b, out_a, out, sems.at[0])
    total, squares = absorb(part_in, norm_in, (got_top, got_low))
    values = (total * lax.rsqrt(squares / features + EPSILON)).astype(BF)
    pltpu.make_async_copy(out_a, out, sems.at[0]).wait()
    score = (middle[...].astype(F32) + matmul(values, out[...])).astype(BF)
    scored[...] = score
    keep = score.shape[0]
    copies = [
        start_copy(scored, repeated.at[pl.ds(place * keep, keep), :], sems.at[1 + place])
        for place in range(repeated.shape[0] // keep)
    ]
    norm[...] = rows_squares[...] + square_sum(score)
    for copy in copies:
        copy.wait()


def share_kernel(share, where, scored, norm, given, value_a, value_b, lout_a, lout_b, *refs):
    every_row, kept, kept_norm, kept_count = refs[:4]
    peers, (value, lout, part, sent, goals, sems) = refs[4:-6], refs[-6:]
    sides = every_row.at[:, pl.ds(scored.shape[1], SIDE)]
    goal_copy = start_copy(sides, goals, sems.at[sems.shape[0] - 1])
    first, at = where[0] == 1, where[1]
    fetch(first, value_b, value_a, value, sems.at[0])
    fetch(first, lout_b, lout_a, lout, sems.at[1])
    inner = value.shape[1]
    score = scored[...]
    sent[:, 2 * inner :] = side_of(norm[...])
    pltpu.make_async_copy(value_a, value, sems.at[0]).wait()
    part[:, :inner] = given[:, :inner] + matmul(score, value[...])
    sent[:, :inner] = part[:, :inner].astype(BF)
    pltpu.make_async_copy(lout_a, lout, sems.at[1]).wait()
    part[:, inner:] = given[:, inner:] + matmul_nt(score, lout[...])
    sent[:, inner : 2 * inner] = part[:, inner:].astype(BF)
    copies = []
    for place, peer in enumerate(peers):
        start = pl.multiple_of((at ^ (place + 1)) * share, share)
        copies.append(start_copy(sent.at[pl.ds(start, share), :], peer, sems.at[2 + place]))
    mine = pl.ds(pl.multiple_of(at * share, share), share)
    kept[...] = part[mine, :]
    kept_norm[...] = norm[mine, :]
    goal_copy.wait()

    def hits(goal):
        shard = 1 + lax.broadcasted_iota(jnp.int32, goal.shape, 1)
        return jnp.where(goal.astype(F32) == shard.astype(F32), 1.0, 0.0)

    counts = jnp.sum(hits(goals[...]), axis=0, keepdims=True)
    row = where[2] * scored.shape[0] + at * share
    own = goals[pl.ds(pl.multiple_of(row, share), share), :]
    kept_count[...] = jnp.maximum(jnp.sum(hits(own) * counts, axis=1, keepdims=True), 1.0)
    for copy in copies:
        copy.wait()


def value_kernel(features, block, count, where, kept, norm, shard_count, *refs):
    got, pieces, crossed = refs[:count], refs[count:-1], refs[-1]
    total, squares = kept[...], norm[...]
    inner = total.shape[1] // 2
    for one in got:
        total = total + one[:, : 2 * inner].astype(F32)
        squares = squares + from_side(one[:, 2 * inner :])
    inverse = lax.rsqrt(squares / features + EPSILON)
    values = (total[:, :inner] * inverse).astype(BF)
    side = side_of(inverse, shard_count[...])
    crossed[...] = total[:, inner:].astype(BF)
    for away, piece in enumerate(pieces):
        if len(pieces) == 1:
            cross = crossed[...]
        else:
            cross = crossed[:, pl.ds(pl.multiple_of((where[0] ^ away) * block, block), block)]
        reach = inner + cross.shape[1]
        piece[:, :inner] = values
        piece[:, inner:reach] = cross
        piece[:, reach:] = side


def gradient_kernel(share, peers, aways, spots, other, where, *refs):
    count = peers * (1 + max(group for group, _ in spots))
    sources, refs = refs[:count], refs[count:]
    every_row, every_scored, lout_in, gram_in, grad_value, grad_out = refs[:6]
    tokens, x, slopes, normed, back, lout, gram, sems = refs[6:]
    first, dp_at, mp_at = where[0] == 1, where[1], where[2]
    take_row = jnp.logical_not(first) if other else first
    keep = share * peers
    width, inner, block = x.shape[1], lout.shape[0], gram.shape[1]
    piece = inner + block + SIDE
    copies = []

    def begin(source, target):
        copies.append(start_copy(source, target, sems.at[len(copies)]))

    begin(lout_in, lout)
    begin(gram_in, gram)
    ready = []
    for number, (away, (group, place)) in enumerate(zip(aways, spots)):
        start = number * keep
        here = pl.ds(pl.multiple_of((dp_at ^ away) * keep, keep), keep)
        target, sem = x.at[pl.ds(start, keep), :], sems.at[len(copies)]
        scored = every_scored.at[here, :]
        fetch(take_row, every_row.at[here, pl.ds(0, width)], scored, target, sem)
        copies.append(pltpu.make_async_copy(scored, target, sem))
        for mask in range(peers):
            at = pl.multiple_of(start + (mp_at ^ mask) * share, share)
            source = sources[group * peers + mask].at[:, pl.ds(place * piece, piece)]
            begin(source, tokens.at[pl.ds(at, share), :])
        ready.append(len(copies))
    done = 0
    for number, until in enumerate(ready):
        for copy in copies[done:until]:
            copy.wait()
        done = until
        here = pl.ds(keep * number, keep)
        wide = x[here, :].astype(F32)
        values = tokens[here, :inner]
        side = tokens[here, inner + block :]
        portion = 1.0 / from_side(side, 1)
        slopes[here, :] = ((wide + matmul(values, lout[...])) * portion).astype(BF)
        normed[here, :] = (wide * from_side(side)).astype(BF)
        crossed = tokens[here, inner : inner + block].astype(F32)
        back[here, :] = ((crossed + matmul(values, gram[...])) * portion).astype(BF)
    column = pl.ds(pl.multiple_of(dp_at * block, block), block)
    grad_value[...] = matmul_tn(back[...], normed[...]).astype(grad_value.dtype)
    grad_out[...] = matmul_tn(tokens[:, column], slopes[...]).astype(grad_out.dtype)


def add_kernel(value_near, out_near, value_far, out_far, grad_value, grad_out):
    grad_value[...] = value_near[...] + value_far[...].astype(F32)
    grad_out[...] = out_near[...] + out_far[...].astype(F32)


def square_sum(value):
    wide = value.astype(F32)
    return jnp.sum(wide * wide, axis=1, keepdims=True)


def exchange(first, second, first_mask, second_mask):
    first, second = lax.optimization_barrier((first, second))
    return lax.optimization_barrier(
        (flip(first, "mp", first_mask), flip(second, "mp", second_mask))
    )


def on_device(
    candidates,
    scorer_value,
    scorer_out,
    learner_value,
    learner_out,
    keep_index,
    keep_dest,
    keep_count,
):
    first = lax.axis_index("segment") == 0
    dp_at = lax.axis_index("dp")
    mp_at = lax.axis_index("mp")
    dp_size = lax.axis_size("dp")
    mp_size = lax.axis_size("mp")
    keep = keep_index.shape[1]
    width = candidates.shape[1]
    scorer_width = width * mp_size
    learner_width = 2 * scorer_width
    inner = learner_value.shape[2]
    block = inner // dp_size
    share = keep // mp_size

    own_value, own_out = scorer_value[0], scorer_out[0]
    own_lvalue, own_lout = learner_value[0], learner_out[0]
    other_value = flip(own_value, "segment", 1)

    is_live = jnp.arange(keep) < keep_count[0]
    pick = (keep_index[0][:, None] == jnp.arange(candidates.shape[0])[None, :]) & is_live[:, None]
    rows = matmul(pick.astype(BF), candidates).astype(BF)
    goal = jnp.where(is_live, keep_dest[0] + 1, 0).astype(F32)[:, None]
    rows_wide = jnp.concatenate([rows, jnp.broadcast_to(goal, (keep, SIDE)).astype(BF)], axis=1)

    def repeat(array):
        return call(
            repeat_kernel,
            [pltpu.HBM((dp_size * keep, array.shape[1]), BF)],
            [VMEM],
            [pltpu.SemaphoreType.DMA((dp_size,))],
            out_specs=[HBM],

        )(array)[0]

    gram = matmul_nt(own_lout, lax.dynamic_slice_in_dim(own_lout, dp_at * block, block, 0))
    half = inner // 2
    at = lax.axis_index("segment")
    kept_half = lax.dynamic_slice_in_dim(gram, at * half, half, 0)
    sent_half = lax.dynamic_slice_in_dim(gram, (1 - at) * half, half, 0)
    got_half = flip(sent_half.astype(BF), "segment", 1)

    direct = dp_size <= 8 and block % SIDE == 0
    flag = first.astype(jnp.int32)
    half_rows = keep // 2
    sums = [jax.ShapeDtypeStruct((keep, inner), F32), jax.ShapeDtypeStruct((keep, 1), F32)]
    state = sums + [jax.ShapeDtypeStruct((half_rows, inner + SIDE), BF)] * 2
    wide_state = state
    if direct:
        extra = half * block // keep
        wide_state = sums + [jax.ShapeDtypeStruct((half_rows, inner + SIDE + extra), BF)] * 2
        wide_state.append(jax.ShapeDtypeStruct((half, block), F32))
    hidden_type = jax.ShapeDtypeStruct((keep, width), BF)
    where = jnp.stack([flag, mp_at, dp_at])
    weight = pltpu.VMEM(own_value.shape, BF)

    def placed(*arrays):
        return [pltpu.with_memory_space_constraint(array, pltpu.HBM) for array in arrays]

    def halves(outs):
        return outs[0], outs[1], outs[2:4], list(outs[4:])

    outs = call(
        functools.partial(start_kernel, direct),
        wide_state,
        [SMEM, VMEM, HBM, HBM] + [VMEM] * (2 * direct),
        [weight, pltpu.SemaphoreType.DMA],
        mebibytes=12,
    )(where, rows, *placed(own_value, other_value), *((kept_half, got_half) if direct else ()))
    part, rows_squares, sents, gram_sum = halves(outs)
    every_row = lax.all_to_all(repeat(rows_wide), "dp", 0, 0, tiled=True)
    own_out, own_lvalue, own_lout, sents = lax.optimization_barrier(
        (own_out, own_lvalue, own_lout, sents)
    )
    other_out = flip(own_out, "segment", 1)
    other_lvalue = flip(own_lvalue, "segment", 1)
    other_lout = flip(own_lout, "segment", 1)
    got = exchange(*sents, 1, 2)
    outs = call(
        functools.partial(between_kernel, direct), wide_state, [VMEM] * (4 + direct), mebibytes=8
    )(part, rows_squares, *got, *gram_sum)
    part, norm, sents, gram_sum = halves(outs)
    got = exchange(*sents, 2, 1)
    outs = call(
        functools.partial(section_kernel, scorer_width, direct),
        [hidden_type] + state + [jax.ShapeDtypeStruct((half, block), BF)] * direct,
        [SMEM] + [VMEM] * 5 + [HBM] * 4 + [VMEM] * direct,
        [weight, weight, pltpu.SemaphoreType.DMA((2,))],
        mebibytes=12,
    )(where, part, norm, *got, rows, *placed(own_out, other_out, own_value, other_value), *gram_sum)
    middle, outs = outs[0], outs[1:]
    part, norm, sents, gram_sum = halves(outs)
    learner_weights = placed(own_lvalue, other_lvalue, own_lout, other_lout)
    given = call(
        learn_kernel,
        [jax.ShapeDtypeStruct((keep, 2 * inner), F32)],
        [SMEM, VMEM] + [HBM] * 4,
        [weight, weight, pltpu.SemaphoreType.DMA((2,))],
        mebibytes=10,
    )(where, rows, *learner_weights)[0]
    got = exchange(*sents, 1, 2)
    outs = call(functools.partial(between_kernel, False), state, [VMEM] * 4)(part, norm, *got)
    part, norm, sents, _ = halves(outs)
    sents, given = lax.optimization_barrier((sents, given))
    got = exchange(*sents, 2, 1)

    long = 2 * inner + SIDE
    scored, norm, repeated = call(
        functools.partial(score_kernel, scorer_width),
        [hidden_type, sums[1], pltpu.HBM((dp_size * keep, width), BF)],
        [SMEM] + [VMEM] * 6 + [HBM] * 2,
        [weight, pltpu.SemaphoreType.DMA((dp_size + 1,))],
        mebibytes=10,
        out_specs=[VMEM, VMEM, HBM],
    )(
        where,
        part,
        norm,
        *got,
        middle,
        rows_squares,
        *placed(own_out, other_out),
    )
    every_scored = lax.all_to_all(repeated, "dp", 0, 0, tiled=True)
    outs = call(
        functools.partial(share_kernel, share),
        [
            jax.ShapeDtypeStruct((share, 2 * inner), F32),
            jax.ShapeDtypeStruct((share, 1), F32),
            jax.ShapeDtypeStruct((share, 1), F32),
        ]
        + [pltpu.HBM((share, long), BF)] * (mp_size - 1),
        [SMEM] + [VMEM] * 3 + [HBM] * 5,
        [
            weight,
            weight,
            pltpu.VMEM((keep, 2 * inner), F32),
            pltpu.VMEM((keep, long), BF),
            pltpu.VMEM((dp_size * keep, SIDE), BF),
            pltpu.SemaphoreType.DMA((mp_size + 2,)),
        ],
        mebibytes=12,
        out_specs=[VMEM] * 3 + [HBM] * (mp_size - 1),
    )(where, scored, norm, given, *learner_weights, every_row)
    kept, kept_norm, shard_count = outs[:3]

    got = lax.optimization_barrier(
        tuple(flip(peer, "mp", mask) for mask, peer in enumerate(outs[3:], 1))
    )
    pieces = call(
        functools.partial(value_kernel, learner_width, block, mp_size - 1),
        [jax.ShapeDtypeStruct((share, inner + block + SIDE), BF)] * dp_size
        if direct
        else [jax.ShapeDtypeStruct((share, long), BF)],
        [SMEM] + [VMEM] * (mp_size + 2),
        [pltpu.VMEM((share, inner), BF)],
    )(jnp.stack([dp_at]), kept, kept_norm, shard_count, *got)

    if direct:
        gram_half = gram_sum[0]
    else:
        gram_half = lax.psum(kept_half + got_half.astype(F32), "mp").astype(BF)
    gram_other = flip(gram_half, "segment", 1)
    gram = jnp.where(
        first,
        jnp.concatenate([gram_half, gram_other], axis=0),
        jnp.concatenate([gram_other, gram_half], axis=0),
    )

    column = dp_at * block

    def spread(piece):
        whole = jnp.zeros((keep, piece.shape[1]), BF)
        for mask in range(mp_size):
            got = flip(piece, "mp", mask) if mask else piece
            whole = lax.dynamic_update_slice(whole, got, ((mp_at ^ mask) * share, 0))
        return whole

    def add(grads, tokens, place):
        v = tokens[:, :inner]
        xo = tokens[:, inner : inner + block].astype(F32)
        inv = unpack(tokens[:, inner + block :], 0)
        share_count = 1.0 / unpack(tokens[:, inner + block :], 1)
        back = ((xo + matmul(v, gram)) * share_count).astype(BF)
        v_block = lax.dynamic_slice_in_dim(v, column, block, 1)
        row = lax.dynamic_slice(every_row, (place * keep, 0), (keep, width))
        score = lax.dynamic_slice_in_dim(every_scored, place * keep, keep, 0)
        added = []
        for x, lout in (
            (jnp.where(first, row, score), own_lout),
            (jnp.where(first, score, row), other_lout),
        ):
            x = x.astype(F32)
            slopes = ((x + matmul(v, lout)) * share_count).astype(BF)
            normed = (x * inv).astype(BF)
            added += [matmul_tn(back, normed), matmul_tn(v_block, slopes)]
        return [grad + new for grad, new in zip(grads, added)]

    if direct:
        moved = [flip(pieces[away], "dp", away) for away in range(1, dp_size)]
        soon = min(3, mp_size)
        own = [pieces[0]] + [flip(pieces[0], "mp", mask) for mask in range(1, soon)]
        moved, own, diagonal = lax.optimization_barrier((moved, own, pieces[0]))
        own += [flip(diagonal, "mp", mask) for mask in range(soon, mp_size)]
        rest = jnp.concatenate(moved, axis=1) if moved else None
        places_at = jnp.stack([flag, dp_at, mp_at])

        def gradients(aways, spots, groups, inputs, other, kind):
            tokens = len(aways) * keep
            return call(
                functools.partial(gradient_kernel, share, mp_size, aways, spots, other),
                [jax.ShapeDtypeStruct((block, width), kind)] * 2,
                [SMEM] + [HBM] * (len(groups) + 4),
                [
                    pltpu.VMEM((tokens, inner + block + SIDE), BF),
                    pltpu.VMEM((tokens, width), BF),
                    pltpu.VMEM((tokens, width), BF),
                    pltpu.VMEM((tokens, width), BF),
                    pltpu.VMEM((tokens, block), BF),
                    pltpu.VMEM(own_lout.shape, BF),
                    pltpu.VMEM(gram.shape, BF),
                    pltpu.SemaphoreType.DMA((len(aways) * (mp_size + 1) + 2,)),
                ],
                mebibytes=16,
            )(places_at, *placed(*groups, *inputs, other_lout if other else own_lout, gram))

        groups, spots = own, ((0, 0),)
        if dp_size > 1:
            groups = own + [rest] + [flip(rest, "mp", mask) for mask in range(1, mp_size)]
            spots += tuple((1, place) for place in range(dp_size - 1))
        inputs = (every_row, every_scored)
        aways = tuple(range(dp_size))
        far = gradients(aways, spots, groups, inputs, True, BF)
        near = gradients(aways, spots, groups, inputs, False, F32)
    else:
        ring = [(source, (source + 1) % dp_size) for source in range(dp_size)]

        def turn(step, carry):
            grads, full = carry
            cross = lax.dynamic_slice_in_dim(full, inner + column, block, 1)
            piece = jnp.concatenate([full[:, :inner], cross, full[:, 2 * inner :]], axis=1)
            grads = add(grads, spread(piece), (dp_at - step) % dp_size)
            return grads, lax.ppermute(full, "dp", ring)

        grads = [jnp.zeros((block, width), F32)] * 4
        grads, _ = lax.fori_loop(0, dp_size, turn, (grads, pieces[0]))
        near, far = grads[:2], [grad.astype(BF) for grad in grads[2:]]
    got = [flip(sent, "segment", 1) for sent in far]
    grads = call(
        add_kernel,
        [jax.ShapeDtypeStruct((block, width), F32)] * 2,
        [VMEM] * 4,
        mebibytes=10,
    )(*near, *got)
    return (grads[0][None], grads[1][None])


def solution(mesh):
    placed = (
        P(("segment", "dp"), "mp"),
        P("segment", "mp", None),
        P("segment", None, "mp"),
        P("segment", "mp", None),
        P("segment", None, "mp"),
        P(("segment", "dp"), None),
        P(("segment", "dp"), None),
        P(("segment", "dp")),
    )
    return jax.shard_map(
        on_device,
        mesh=mesh,
        in_specs=placed,
        out_specs=(P("segment", "dp", "mp"), P("segment", "dp", "mp")),
        check_vma=False,
    )
```

```python
import functools

import jax
import jax.numpy as jnp
from jax import lax
from jax.experimental import pallas as pl
from jax.experimental.pallas import tpu as pltpu
from jax.sharding import PartitionSpec as P

EPSILON = 1e-05
BF = jnp.bfloat16
F32 = jnp.float32
SIDE = 128


def flip(value, axis, mask):
    pairs = [(source, source ^ mask) for source in range(lax.axis_size(axis))]
    return lax.ppermute(value, axis, pairs)


def matmul(left, right):
    return jnp.dot(left, right, preferred_element_type=F32)


def matmul_nt(left, right):
    return lax.dot_general(left, right, (((1,), (1,)), ((), ())), preferred_element_type=F32)


def matmul_tn(left, right):
    return lax.dot_general(left, right, (((0,), (0,)), ((), ())), preferred_element_type=F32)


def unpack(side, place):
    wide = side[:, 3 * place : 3 * place + 3].astype(F32)
    return wide[:, 0:1] + wide[:, 1:2] + wide[:, 2:3]


VMEM = pl.BlockSpec(memory_space=pltpu.VMEM)
SMEM = pl.BlockSpec(memory_space=pltpu.SMEM)
HBM = pl.BlockSpec(memory_space=pltpu.HBM)


def call(body, outs, in_specs, scratch=(), mebibytes=4, out_specs=None, cost=None):
    return pl.pallas_call(
        body,
        out_shape=outs,
        in_specs=in_specs,
        out_specs=out_specs or [VMEM] * len(outs),
        scratch_shapes=list(scratch),
        compiler_params=pltpu.CompilerParams(vmem_limit_bytes=mebibytes << 20),
        cost_estimate=cost,
    )


def fetch(take_left, left, right, target, sem):
    @pl.when(take_left)
    def _():
        pltpu.make_async_copy(left, target, sem).start()

    @pl.when(jnp.logical_not(take_left))
    def _():
        pltpu.make_async_copy(right, target, sem).start()


def start_copy(source, target, sem):
    copy = pltpu.make_async_copy(source, target, sem)
    copy.start()
    return copy


def side_of(*columns):
    lane = lax.broadcasted_iota(jnp.int32, (columns[0].shape[0], SIDE), 1)
    picked = jnp.zeros(lane.shape, F32)
    for place, column in enumerate(columns):
        high = column.astype(BF).astype(F32)
        middle = (column - high).astype(BF).astype(F32)
        for part, piece in enumerate((high, middle, column - high - middle)):
            picked = jnp.where(lane == 3 * place + part, piece, picked)
    return picked.astype(BF)


def from_side(side, place=0):
    lane = lax.broadcasted_iota(jnp.int32, side.shape, 1)
    own = (lane >= 3 * place) & (lane < 3 * place + 3)
    return jnp.sum(jnp.where(own, side.astype(F32), 0.0), axis=1, keepdims=True)


def emit(part, norm, sents, gram=None):
    half, width = sents[0].shape[0], part.shape[1]
    for place, sent in enumerate(sents):
        start = place * half
        sent[:, :width] = part[start : start + half, :].astype(BF)
        sent[:, width : width + SIDE] = side_of(norm[start : start + half, :])
        if gram is not None:
            for rows, columns in gram_blocks(gram, place, half, width):
                sent[:, columns] = gram[rows, :].astype(BF)


def gram_blocks(gram, place, half, width):
    count, block = gram.shape[0] // 2 // half, gram.shape[1]
    for index in range(count):
        row = (place * count + index) * half
        column = width + SIDE + index * block
        yield slice(row, row + half), slice(column, column + block)


def absorb(part, norm, gots, gram=None, gram_sum=None):
    half, width = gots[0].shape[0], part.shape[1]
    parts, norms = [], []
    for place, got in enumerate(gots):
        start = place * half
        parts.append(part[start : start + half, :] + got[:, :width].astype(F32))
        side = got[:, width : width + SIDE]
        norms.append(norm[start : start + half, :] + from_side(side))
        if gram is not None:
            for rows, columns in gram_blocks(gram, place, half, width):
                summed = gram[rows, :] + got[:, columns].astype(F32)
                gram_sum[rows, :] = summed.astype(gram_sum.dtype)
    return jnp.concatenate(parts, axis=0), jnp.concatenate(norms, axis=0)


def repeat_kernel(array, repeated, sems):
    rows = array.shape[0]
    copies = [
        start_copy(array, repeated.at[pl.ds(place * rows, rows), :], sems.at[place])
        for place in range(repeated.shape[0] // rows)
    ]
    for copy in copies:
        copy.wait()


def start_kernel(with_gram, where, rows, value_a, value_b, *refs):
    gram_a, gram_b = refs[:2] if with_gram else (None, None)
    refs = refs[2:] if with_gram else refs
    part, norm, top, low = refs[:4]
    gram, (weight, sem) = refs[4] if with_gram else None, refs[-2:]
    fetch(where[0] == 1, value_a, value_b, weight, sem)
    row = rows[...]
    norm[...] = square_sum(row)
    if with_gram:
        gram[...] = gram_a[...] + gram_b[...].astype(F32)
    pltpu.make_async_copy(value_a, weight, sem).wait()
    part[...] = matmul(row, weight[...])
    emit(part, norm, (top, low), gram)


def between_kernel(with_gram, part_in, norm_in, got_top, got_low, *refs):
    gram_in, refs = (refs[0], refs[1:]) if with_gram else (None, refs)
    part, norm, top, low = refs[:4]
    gram = refs[4] if with_gram else None
    part[...], norm[...] = absorb(part_in, norm_in, (got_top, got_low), gram_in, gram)
    emit(part, norm, (top, low), gram)


def section_kernel(features, with_gram, where, *refs):
    part_in, norm_in, got_top, got_low, rows, out_a, out_b, value_a, value_b = refs[:9]
    gram_in, refs = (refs[9], refs[10:]) if with_gram else (None, refs[9:])
    middle, part, norm, top, low = refs[:5]
    gram, (out, value, sems) = refs[5] if with_gram else None, refs[-3:]
    first = where[0] == 1
    fetch(first, out_a, out_b, out, sems.at[0])
    fetch(first, value_b, value_a, value, sems.at[1])
    total, squares = absorb(part_in, norm_in, (got_top, got_low), gram_in, gram)
    values = (total * lax.rsqrt(squares / features + EPSILON)).astype(BF)
    pltpu.make_async_copy(out_a, out, sems.at[0]).wait()
    hidden = (rows[...].astype(F32) + matmul(values, out[...])).astype(BF)
    middle[...] = hidden
    norm[...] = square_sum(hidden)
    pltpu.make_async_copy(value_a, value, sems.at[1]).wait()
    part[...] = matmul(hidden, value[...])
    emit(part, norm, (top, low))


def learn_kernel(where, rows, value_a, value_b, lout_a, lout_b, part, value, lout, sems):
    first = where[0] == 1
    fetch(first, value_a, value_b, value, sems.at[0])
    fetch(first, lout_a, lout_b, lout, sems.at[1])
    inner = value.shape[1]
    pltpu.make_async_copy(value_a, value, sems.at[0]).wait()
    part[:, :inner] = matmul(rows[...], value[...])
    pltpu.make_async_copy(lout_a, lout, sems.at[1]).wait()
    part[:, inner:] = matmul_nt(rows[...], lout[...])


def score_kernel(features, where, *refs):
    part_in, norm_in, got_top, got_low, middle, rows_squares, out_a, out_b = refs[:8]
    scored, norm, repeated, out, sems = refs[8:]
    fetch(where[0] == 1, out_b, out_a, out, sems.at[0])
    total, squares = absorb(part_in, norm_in, (got_top, got_low))
    values = (total * lax.rsqrt(squares / features + EPSILON)).astype(BF)
    pltpu.make_async_copy(out_a, out, sems.at[0]).wait()
    score = (middle[...].astype(F32) + matmul(values, out[...])).astype(BF)
    scored[...] = score
    keep = score.shape[0]
    copies = [
        start_copy(scored, repeated.at[pl.ds(place * keep, keep), :], sems.at[1 + place])
        for place in range(repeated.shape[0] // keep)
    ]
    norm[...] = rows_squares[...] + square_sum(score)
    for copy in copies:
        copy.wait()


def share_kernel(share, where, scored, norm, given, value_a, value_b, lout_a, lout_b, *refs):
    every_row, kept, kept_norm, kept_count = refs[:4]
    peers, (value, lout, part, sent, goals, sems) = refs[4:-6], refs[-6:]
    sides = every_row.at[:, pl.ds(scored.shape[1], SIDE)]
    goal_copy = start_copy(sides, goals, sems.at[sems.shape[0] - 1])
    first, at = where[0] == 1, where[1]
    fetch(first, value_b, value_a, value, sems.at[0])
    fetch(first, lout_b, lout_a, lout, sems.at[1])
    inner = value.shape[1]
    score = scored[...]
    sent[:, 2 * inner :] = side_of(norm[...])
    pltpu.make_async_copy(value_a, value, sems.at[0]).wait()
    part[:, :inner] = given[:, :inner] + matmul(score, value[...])
    sent[:, :inner] = part[:, :inner].astype(BF)
    pltpu.make_async_copy(lout_a, lout, sems.at[1]).wait()
    part[:, inner:] = given[:, inner:] + matmul_nt(score, lout[...])
    sent[:, inner : 2 * inner] = part[:, inner:].astype(BF)
    copies = []
    for place, peer in enumerate(peers):
        start = pl.multiple_of((at ^ (place + 1)) * share, share)
        copies.append(start_copy(sent.at[pl.ds(start, share), :], peer, sems.at[2 + place]))
    mine = pl.ds(pl.multiple_of(at * share, share), share)
    kept[...] = part[mine, :]
    kept_norm[...] = norm[mine, :]
    goal_copy.wait()

    def hits(goal):
        shard = 1 + lax.broadcasted_iota(jnp.int32, goal.shape, 1)
        return jnp.where(goal.astype(F32) == shard.astype(F32), 1.0, 0.0)

    counts = jnp.sum(hits(goals[...]), axis=0, keepdims=True)
    row = where[2] * scored.shape[0] + at * share
    own = goals[pl.ds(pl.multiple_of(row, share), share), :]
    kept_count[...] = jnp.maximum(jnp.sum(hits(own) * counts, axis=1, keepdims=True), 1.0)
    for copy in copies:
        copy.wait()


def value_kernel(features, block, count, where, kept, norm, shard_count, *refs):
    got, pieces, crossed = refs[:count], refs[count:-1], refs[-1]
    total, squares = kept[...], norm[...]
    inner = total.shape[1] // 2
    for one in got:
        total = total + one[:, : 2 * inner].astype(F32)
        squares = squares + from_side(one[:, 2 * inner :])
    inverse = lax.rsqrt(squares / features + EPSILON)
    values = (total[:, :inner] * inverse).astype(BF)
    side = side_of(inverse, shard_count[...])
    crossed[...] = total[:, inner:].astype(BF)
    for away, piece in enumerate(pieces):
        if len(pieces) == 1:
            cross = crossed[...]
        else:
            cross = crossed[:, pl.ds(pl.multiple_of((where[0] ^ away) * block, block), block)]
        reach = inner + cross.shape[1]
        piece[:, :inner] = values
        piece[:, inner:reach] = cross
        piece[:, reach:] = side


def gradient_kernel(share, peers, aways, spots, other, where, *refs):
    count = peers * (1 + max(group for group, _ in spots))
    sources, refs = refs[:count], refs[count:]
    every_row, every_scored, lout_in, gram_in, grad_value, grad_out = refs[:6]
    tokens, x, slopes, normed, back, lout, gram, sems = refs[6:]
    first, dp_at, mp_at = where[0] == 1, where[1], where[2]
    take_row = jnp.logical_not(first) if other else first
    keep = share * peers
    width, inner, block = x.shape[1], lout.shape[0], gram.shape[1]
    piece = inner + block + SIDE
    copies = []

    def begin(source, target):
        copies.append(start_copy(source, target, sems.at[len(copies)]))

    ready = []
    for number, (away, (group, place)) in enumerate(zip(aways, spots)):
        start = number * keep
        here = pl.ds(pl.multiple_of((dp_at ^ away) * keep, keep), keep)
        target, sem = x.at[pl.ds(start, keep), :], sems.at[len(copies)]
        scored = every_scored.at[here, :]
        fetch(take_row, every_row.at[here, pl.ds(0, width)], scored, target, sem)
        copies.append(pltpu.make_async_copy(scored, target, sem))
        for mask in range(peers):
            at = pl.multiple_of(start + (mp_at ^ mask) * share, share)
            source = sources[group * peers + mask].at[:, pl.ds(place * piece, piece)]
            begin(source, tokens.at[pl.ds(at, share), :])
        ready.append(len(copies))
        if number == min(1, len(aways) - 1):
            maps = len(copies)
            begin(gram_in, gram)
            begin(lout_in, lout)
    done, step = 0, 2 if len(aways) % 2 == 0 else 1
    for number in range(0, len(aways), step):
        until = ready[number + step - 1]
        for index in range(done, until):
            if index not in (maps, maps + 1):
                copies[index].wait()
        done = until
        here = pl.ds(keep * number, keep * step)
        wide = x[here, :].astype(F32)
        side = tokens[here, inner + block :]
        portion = 1.0 / from_side(side, 1)
        normed[here, :] = (wide * from_side(side)).astype(BF)
        values = tokens[here, :inner]
        crossed = tokens[here, inner : inner + block].astype(F32)
        if number == 0:
            copies[maps].wait()
        back[here, :] = ((crossed + matmul(values, gram[...])) * portion).astype(BF)
        if number == 0:
            copies[maps + 1].wait()
        slopes[here, :] = ((wide + matmul(values, lout[...])) * portion).astype(BF)
    column = pl.ds(pl.multiple_of(dp_at * block, block), block)
    grad_value[...] = matmul_tn(back[...], normed[...]).astype(grad_value.dtype)
    grad_out[...] = matmul_tn(tokens[:, column], slopes[...]).astype(grad_out.dtype)


def add_kernel(value_near, out_near, value_far, out_far, grad_value, grad_out):
    grad_value[...] = value_near[...] + value_far[...].astype(F32)
    grad_out[...] = out_near[...] + out_far[...].astype(F32)


def square_sum(value):
    wide = value.astype(F32)
    return jnp.sum(wide * wide, axis=1, keepdims=True)


def exchange(first, second, first_mask, second_mask):
    first, second = lax.optimization_barrier((first, second))
    return lax.optimization_barrier(
        (flip(first, "mp", first_mask), flip(second, "mp", second_mask))
    )


def on_device(
    candidates,
    scorer_value,
    scorer_out,
    learner_value,
    learner_out,
    keep_index,
    keep_dest,
    keep_count,
):
    first = lax.axis_index("segment") == 0
    dp_at = lax.axis_index("dp")
    mp_at = lax.axis_index("mp")
    dp_size = lax.axis_size("dp")
    mp_size = lax.axis_size("mp")
    keep = keep_index.shape[1]
    width = candidates.shape[1]
    scorer_width = width * mp_size
    learner_width = 2 * scorer_width
    inner = learner_value.shape[2]
    block = inner // dp_size
    share = keep // mp_size

    own_value, own_out = scorer_value[0], scorer_out[0]
    own_lvalue, own_lout = learner_value[0], learner_out[0]
    other_value = flip(own_value, "segment", 1)

    is_live = jnp.arange(keep) < keep_count[0]
    pick = (keep_index[0][:, None] == jnp.arange(candidates.shape[0])[None, :]) & is_live[:, None]
    rows = matmul(pick.astype(BF), candidates).astype(BF)
    goal = jnp.where(is_live, keep_dest[0] + 1, 0).astype(F32)[:, None]
    rows_wide = jnp.concatenate([rows, jnp.broadcast_to(goal, (keep, SIDE)).astype(BF)], axis=1)

    def repeat(array):
        return call(
            repeat_kernel,
            [pltpu.HBM((dp_size * keep, array.shape[1]), BF)],
            [VMEM],
            [pltpu.SemaphoreType.DMA((dp_size,))],
            out_specs=[HBM],
        )(array)[0]

    gram = matmul_nt(own_lout, lax.dynamic_slice_in_dim(own_lout, dp_at * block, block, 0))
    half = inner // 2
    at = lax.axis_index("segment")
    kept_half = lax.dynamic_slice_in_dim(gram, at * half, half, 0)
    sent_half = lax.dynamic_slice_in_dim(gram, (1 - at) * half, half, 0)
    got_half = flip(sent_half.astype(BF), "segment", 1)

    direct = dp_size <= 8 and block % SIDE == 0
    flag = first.astype(jnp.int32)
    half_rows = keep // 2
    sums = [jax.ShapeDtypeStruct((keep, inner), F32), jax.ShapeDtypeStruct((keep, 1), F32)]
    state = sums + [jax.ShapeDtypeStruct((half_rows, inner + SIDE), BF)] * 2
    wide_state = state
    if direct:
        extra = half * block // keep
        wide_state = sums + [jax.ShapeDtypeStruct((half_rows, inner + SIDE + extra), BF)] * 2
        wide_state.append(jax.ShapeDtypeStruct((half, block), F32))
    hidden_type = jax.ShapeDtypeStruct((keep, width), BF)
    where = jnp.stack([flag, mp_at, dp_at])
    weight = pltpu.VMEM(own_value.shape, BF)

    def placed(*arrays):
        return [pltpu.with_memory_space_constraint(array, pltpu.HBM) for array in arrays]

    def halves(outs):
        return outs[0], outs[1], outs[2:4], list(outs[4:])

    outs = call(
        functools.partial(start_kernel, direct),
        wide_state,
        [SMEM, VMEM, HBM, HBM] + [VMEM] * (2 * direct),
        [weight, pltpu.SemaphoreType.DMA],
        mebibytes=12,
    )(where, rows, *placed(own_value, other_value), *((kept_half, got_half) if direct else ()))
    part, rows_squares, sents, gram_sum = halves(outs)
    every_row = lax.all_to_all(repeat(rows_wide), "dp", 0, 0, tiled=True)
    own_out, own_lvalue, own_lout, sents = lax.optimization_barrier(
        (own_out, own_lvalue, own_lout, sents)
    )
    other_out = flip(own_out, "segment", 1)
    other_lvalue = flip(own_lvalue, "segment", 1)
    other_lout = flip(own_lout, "segment", 1)
    got = exchange(*sents, 1, 2)
    outs = call(
        functools.partial(between_kernel, direct), wide_state, [VMEM] * (4 + direct), mebibytes=8
    )(part, rows_squares, *got, *gram_sum)
    part, norm, sents, gram_sum = halves(outs)
    got = exchange(*sents, 2, 1)
    outs = call(
        functools.partial(section_kernel, scorer_width, direct),
        [hidden_type] + state + [jax.ShapeDtypeStruct((half, block), BF)] * direct,
        [SMEM] + [VMEM] * 5 + [HBM] * 4 + [VMEM] * direct,
        [weight, weight, pltpu.SemaphoreType.DMA((2,))],
        mebibytes=12,
    )(where, part, norm, *got, rows, *placed(own_out, other_out, own_value, other_value), *gram_sum)
    middle, outs = outs[0], outs[1:]
    part, norm, sents, gram_sum = halves(outs)
    learner_weights = placed(own_lvalue, other_lvalue, own_lout, other_lout)
    given = call(
        learn_kernel,
        [jax.ShapeDtypeStruct((keep, 2 * inner), F32)],
        [SMEM, VMEM] + [HBM] * 4,
        [weight, weight, pltpu.SemaphoreType.DMA((2,))],
        mebibytes=10,
    )(where, rows, *learner_weights)[0]
    got = exchange(*sents, 1, 2)
    outs = call(functools.partial(between_kernel, False), state, [VMEM] * 4)(part, norm, *got)
    part, norm, sents, _ = halves(outs)
    sents, given = lax.optimization_barrier((sents, given))
    got = exchange(*sents, 2, 1)

    long = 2 * inner + SIDE
    scored, norm, repeated = call(
        functools.partial(score_kernel, scorer_width),
        [hidden_type, sums[1], pltpu.HBM((dp_size * keep, width), BF)],
        [SMEM] + [VMEM] * 6 + [HBM] * 2,
        [weight, pltpu.SemaphoreType.DMA((dp_size + 1,))],
        mebibytes=10,
        out_specs=[VMEM, VMEM, HBM],
    )(
        where,
        part,
        norm,
        *got,
        middle,
        rows_squares,
        *placed(own_out, other_out),
    )
    every_scored = lax.all_to_all(repeated, "dp", 0, 0, tiled=True)
    outs = call(
        functools.partial(share_kernel, share),
        [
            jax.ShapeDtypeStruct((share, 2 * inner), F32),
            jax.ShapeDtypeStruct((share, 1), F32),
            jax.ShapeDtypeStruct((share, 1), F32),
        ]
        + [pltpu.HBM((share, long), BF)] * (mp_size - 1),
        [SMEM] + [VMEM] * 3 + [HBM] * 5,
        [
            weight,
            weight,
            pltpu.VMEM((keep, 2 * inner), F32),
            pltpu.VMEM((keep, long), BF),
            pltpu.VMEM((dp_size * keep, SIDE), BF),
            pltpu.SemaphoreType.DMA((mp_size + 2,)),
        ],
        mebibytes=12,
        out_specs=[VMEM] * 3 + [HBM] * (mp_size - 1),
    )(where, scored, norm, given, *learner_weights, every_row)
    kept, kept_norm, shard_count = outs[:3]

    got = lax.optimization_barrier(
        tuple(flip(peer, "mp", mask) for mask, peer in enumerate(outs[3:], 1))
    )
    pieces = call(
        functools.partial(value_kernel, learner_width, block, mp_size - 1),
        [jax.ShapeDtypeStruct((share, inner + block + SIDE), BF)] * dp_size
        if direct
        else [jax.ShapeDtypeStruct((share, long), BF)],
        [SMEM] + [VMEM] * (mp_size + 2),
        [pltpu.VMEM((share, inner), BF)],
    )(jnp.stack([dp_at]), kept, kept_norm, shard_count, *got)

    if direct:
        gram_half = gram_sum[0]
    else:
        gram_half = lax.psum(kept_half + got_half.astype(F32), "mp").astype(BF)
    gram_other = flip(gram_half, "segment", 1)
    gram = jnp.where(
        first,
        jnp.concatenate([gram_half, gram_other], axis=0),
        jnp.concatenate([gram_other, gram_half], axis=0),
    )

    column = dp_at * block

    def spread(piece):
        whole = jnp.zeros((keep, piece.shape[1]), BF)
        for mask in range(mp_size):
            got = flip(piece, "mp", mask) if mask else piece
            whole = lax.dynamic_update_slice(whole, got, ((mp_at ^ mask) * share, 0))
        return whole

    def add(grads, tokens, place):
        v = tokens[:, :inner]
        xo = tokens[:, inner : inner + block].astype(F32)
        inv = unpack(tokens[:, inner + block :], 0)
        share_count = 1.0 / unpack(tokens[:, inner + block :], 1)
        back = ((xo + matmul(v, gram)) * share_count).astype(BF)
        v_block = lax.dynamic_slice_in_dim(v, column, block, 1)
        row = lax.dynamic_slice(every_row, (place * keep, 0), (keep, width))
        score = lax.dynamic_slice_in_dim(every_scored, place * keep, keep, 0)
        added = []
        for x, lout in (
            (jnp.where(first, row, score), own_lout),
            (jnp.where(first, score, row), other_lout),
        ):
            x = x.astype(F32)
            slopes = ((x + matmul(v, lout)) * share_count).astype(BF)
            normed = (x * inv).astype(BF)
            added += [matmul_tn(back, normed), matmul_tn(v_block, slopes)]
        return [grad + new for grad, new in zip(grads, added)]

    if direct:
        moved = [flip(pieces[away], "dp", away) for away in range(1, dp_size)]
        soon = min(3, mp_size)
        own = [pieces[0]] + [flip(pieces[0], "mp", mask) for mask in range(1, soon)]
        moved, own, diagonal = lax.optimization_barrier((moved, own, pieces[0]))
        own += [flip(diagonal, "mp", mask) for mask in range(soon, mp_size)]
        rest = jnp.concatenate(moved, axis=1) if moved else None
        places_at = jnp.stack([flag, dp_at, mp_at])

        def gradients(aways, spots, groups, inputs, other, kind):
            tokens = len(aways) * keep
            return call(
                functools.partial(gradient_kernel, share, mp_size, aways, spots, other),
                [jax.ShapeDtypeStruct((block, width), kind)] * 2,
                [SMEM] + [HBM] * (len(groups) + 4),
                [
                    pltpu.VMEM((tokens, inner + block + SIDE), BF),
                    pltpu.VMEM((tokens, width), BF),
                    pltpu.VMEM((tokens, width), BF),
                    pltpu.VMEM((tokens, width), BF),
                    pltpu.VMEM((tokens, block), BF),
                    pltpu.VMEM(own_lout.shape, BF),
                    pltpu.VMEM(gram.shape, BF),
                    pltpu.SemaphoreType.DMA((len(aways) * (mp_size + 1) + 2,)),
                ],
                mebibytes=16,
            )(places_at, *placed(*groups, *inputs, other_lout if other else own_lout, gram))

        groups, spots = own, ((0, 0),)
        if dp_size > 1:
            groups = own + [rest] + [flip(rest, "mp", mask) for mask in range(1, mp_size)]
            spots += tuple((1, place) for place in range(dp_size - 1))
        inputs = (every_row, every_scored)
        aways = tuple(range(dp_size))
        far = gradients(aways, spots, groups, inputs, True, BF)
        near = gradients(aways, spots, groups, inputs, False, F32)
    else:
        ring = [(source, (source + 1) % dp_size) for source in range(dp_size)]

        def turn(step, carry):
            grads, full = carry
            cross = lax.dynamic_slice_in_dim(full, inner + column, block, 1)
            piece = jnp.concatenate([full[:, :inner], cross, full[:, 2 * inner :]], axis=1)
            grads = add(grads, spread(piece), (dp_at - step) % dp_size)
            return grads, lax.ppermute(full, "dp", ring)

        grads = [jnp.zeros((block, width), F32)] * 4
        grads, _ = lax.fori_loop(0, dp_size, turn, (grads, pieces[0]))
        near, far = grads[:2], [grad.astype(BF) for grad in grads[2:]]
    got = [flip(sent, "segment", 1) for sent in far]
    grads = call(
        add_kernel,
        [jax.ShapeDtypeStruct((block, width), F32)] * 2,
        [VMEM] * 4,
        mebibytes=10,
    )(*near, *got)
    return (grads[0][None], grads[1][None])


def solution(mesh):
    placed = (
        P(("segment", "dp"), "mp"),
        P("segment", "mp", None),
        P("segment", None, "mp"),
        P("segment", "mp", None),
        P("segment", None, "mp"),
        P(("segment", "dp"), None),
        P(("segment", "dp"), None),
        P(("segment", "dp")),
    )
    return jax.shard_map(
        on_device,
        mesh=mesh,
        in_specs=placed,
        out_specs=(P("segment", "dp", "mp"), P("segment", "dp", "mp")),
        check_vma=False,
    )
```

```python
import functools

import jax
import jax.numpy as jnp
from jax import lax
from jax.experimental import pallas as pl
from jax.experimental.pallas import tpu as pltpu
from jax.sharding import PartitionSpec as P

EPSILON = 1e-05
BF = jnp.bfloat16
F32 = jnp.float32
SIDE = 128


def flip(value, axis, mask):
    pairs = [(source, source ^ mask) for source in range(lax.axis_size(axis))]
    return lax.ppermute(value, axis, pairs)


def matmul(left, right):
    return jnp.dot(left, right, preferred_element_type=F32)


def matmul_nt(left, right):
    return lax.dot_general(left, right, (((1,), (1,)), ((), ())), preferred_element_type=F32)


def matmul_tn(left, right):
    return lax.dot_general(left, right, (((0,), (0,)), ((), ())), preferred_element_type=F32)


def unpack(side, place):
    wide = side[:, 3 * place : 3 * place + 3].astype(F32)
    return wide[:, 0:1] + wide[:, 1:2] + wide[:, 2:3]


VMEM = pl.BlockSpec(memory_space=pltpu.VMEM)
SMEM = pl.BlockSpec(memory_space=pltpu.SMEM)
HBM = pl.BlockSpec(memory_space=pltpu.HBM)


def call(body, outs, in_specs, scratch=(), mebibytes=12, out_specs=None, cost=None):
    return pl.pallas_call(
        body,
        out_shape=outs,
        in_specs=in_specs,
        out_specs=out_specs or [VMEM] * len(outs),
        scratch_shapes=list(scratch),
        compiler_params=pltpu.CompilerParams(vmem_limit_bytes=mebibytes << 20),
        cost_estimate=cost,
    )


def fetch(take_left, left, right, target, sem):
    @pl.when(take_left)
    def _():
        pltpu.make_async_copy(left, target, sem).start()

    @pl.when(jnp.logical_not(take_left))
    def _():
        pltpu.make_async_copy(right, target, sem).start()


def start_copy(source, target, sem):
    copy = pltpu.make_async_copy(source, target, sem)
    copy.start()
    return copy


def side_of(*columns):
    lane = lax.broadcasted_iota(jnp.int32, (columns[0].shape[0], SIDE), 1)
    picked = jnp.zeros(lane.shape, F32)
    for place, column in enumerate(columns):
        high = column.astype(BF).astype(F32)
        middle = (column - high).astype(BF).astype(F32)
        for part, piece in enumerate((high, middle, column - high - middle)):
            picked = jnp.where(lane == 3 * place + part, piece, picked)
    return picked.astype(BF)


def from_side(side, place=0):
    lane = lax.broadcasted_iota(jnp.int32, side.shape, 1)
    own = (lane >= 3 * place) & (lane < 3 * place + 3)
    return jnp.sum(jnp.where(own, side.astype(F32), 0.0), axis=1, keepdims=True)


def emit(part, norm, sents, gram=None):
    half, width = sents[0].shape[0], part.shape[1]
    for place, sent in enumerate(sents):
        start = place * half
        sent[:, :width] = part[start : start + half, :].astype(BF)
        sent[:, width : width + SIDE] = side_of(norm[start : start + half, :])
        if gram is not None:
            for rows, columns in gram_blocks(gram, place, half, width):
                sent[:, columns] = gram[rows, :].astype(BF)


def gram_blocks(gram, place, half, width):
    count, block = gram.shape[0] // 2 // half, gram.shape[1]
    for index in range(count):
        row = (place * count + index) * half
        column = width + SIDE + index * block
        yield slice(row, row + half), slice(column, column + block)


def absorb(part, norm, gots, gram=None, gram_sum=None):
    half, width = gots[0].shape[0], part.shape[1]
    parts, norms = [], []
    for place, got in enumerate(gots):
        start = place * half
        parts.append(part[start : start + half, :] + got[:, :width].astype(F32))
        side = got[:, width : width + SIDE]
        norms.append(norm[start : start + half, :] + from_side(side))
        if gram is not None:
            for rows, columns in gram_blocks(gram, place, half, width):
                summed = gram[rows, :] + got[:, columns].astype(F32)
                gram_sum[rows, :] = summed.astype(gram_sum.dtype)
    return jnp.concatenate(parts, axis=0), jnp.concatenate(norms, axis=0)


def repeat_kernel(array, repeated, sems):
    rows = array.shape[0]
    copies = [
        start_copy(array, repeated.at[pl.ds(place * rows, rows), :], sems.at[place])
        for place in range(repeated.shape[0] // rows)
    ]
    for copy in copies:
        copy.wait()


def start_kernel(with_gram, where, rows, value_a, value_b, *refs):
    gram_a, gram_b = refs[:2] if with_gram else (None, None)
    refs = refs[2:] if with_gram else refs
    part, norm, top, low = refs[:4]
    gram, (weight, sem) = refs[4] if with_gram else None, refs[-2:]
    fetch(where[0] == 1, value_a, value_b, weight, sem)
    row = rows[...]
    norm[...] = square_sum(row)
    if with_gram:
        gram[...] = gram_a[...] + gram_b[...].astype(F32)
    pltpu.make_async_copy(value_a, weight, sem).wait()
    part[...] = matmul(row, weight[...])
    emit(part, norm, (top, low), gram)


def between_kernel(with_gram, part_in, norm_in, got_top, got_low, *refs):
    gram_in, refs = (refs[0], refs[1:]) if with_gram else (None, refs)
    part, norm, top, low = refs[:4]
    gram = refs[4] if with_gram else None
    part[...], norm[...] = absorb(part_in, norm_in, (got_top, got_low), gram_in, gram)
    emit(part, norm, (top, low), gram)


def section_kernel(features, with_gram, where, *refs):
    part_in, norm_in, got_top, got_low, rows, out_a, out_b, value_a, value_b = refs[:9]
    gram_in, refs = (refs[9], refs[10:]) if with_gram else (None, refs[9:])
    middle, part, norm, top, low = refs[:5]
    gram, (out, value, sems) = refs[5] if with_gram else None, refs[-3:]
    first = where[0] == 1
    fetch(first, out_a, out_b, out, sems.at[0])
    fetch(first, value_b, value_a, value, sems.at[1])
    total, squares = absorb(part_in, norm_in, (got_top, got_low), gram_in, gram)
    values = (total * lax.rsqrt(squares / features + EPSILON)).astype(BF)
    pltpu.make_async_copy(out_a, out, sems.at[0]).wait()
    hidden = (rows[...].astype(F32) + matmul(values, out[...])).astype(BF)
    middle[...] = hidden
    norm[...] = square_sum(hidden)
    pltpu.make_async_copy(value_a, value, sems.at[1]).wait()
    part[...] = matmul(hidden, value[...])
    emit(part, norm, (top, low))


def learn_kernel(where, rows, value_a, value_b, lout_a, lout_b, part, value, lout, sems):
    first = where[0] == 1
    fetch(first, value_a, value_b, value, sems.at[0])
    fetch(first, lout_a, lout_b, lout, sems.at[1])
    inner = value.shape[1]
    pltpu.make_async_copy(value_a, value, sems.at[0]).wait()
    part[:, :inner] = matmul(rows[...], value[...])
    pltpu.make_async_copy(lout_a, lout, sems.at[1]).wait()
    part[:, inner:] = matmul_nt(rows[...], lout[...])


def score_kernel(features, where, *refs):
    part_in, norm_in, got_top, got_low, middle, rows_squares, out_a, out_b = refs[:8]
    scored, norm, repeated, out, sems = refs[8:]
    fetch(where[0] == 1, out_b, out_a, out, sems.at[0])
    total, squares = absorb(part_in, norm_in, (got_top, got_low))
    values = (total * lax.rsqrt(squares / features + EPSILON)).astype(BF)
    pltpu.make_async_copy(out_a, out, sems.at[0]).wait()
    score = (middle[...].astype(F32) + matmul(values, out[...])).astype(BF)
    scored[...] = score
    keep = score.shape[0]
    copies = [
        start_copy(scored, repeated.at[pl.ds(place * keep, keep), :], sems.at[1 + place])
        for place in range(repeated.shape[0] // keep)
    ]
    norm[...] = rows_squares[...] + square_sum(score)
    for copy in copies:
        copy.wait()


def share_kernel(share, where, scored, norm, given, value_a, value_b, lout_a, lout_b, *refs):
    every_row, kept, kept_norm, kept_count = refs[:4]
    peers, (value, lout, part, sent, goals, sems) = refs[4:-6], refs[-6:]
    sides = every_row.at[:, pl.ds(scored.shape[1], SIDE)]
    goal_copy = start_copy(sides, goals, sems.at[sems.shape[0] - 1])
    first, at = where[0] == 1, where[1]
    fetch(first, value_b, value_a, value, sems.at[0])
    fetch(first, lout_b, lout_a, lout, sems.at[1])
    inner = value.shape[1]
    score = scored[...]
    sent[:, 2 * inner :] = side_of(norm[...])
    pltpu.make_async_copy(value_a, value, sems.at[0]).wait()
    part[:, :inner] = given[:, :inner] + matmul(score, value[...])
    sent[:, :inner] = part[:, :inner].astype(BF)
    pltpu.make_async_copy(lout_a, lout, sems.at[1]).wait()
    part[:, inner:] = given[:, inner:] + matmul_nt(score, lout[...])
    sent[:, inner : 2 * inner] = part[:, inner:].astype(BF)
    copies = []
    for place, peer in enumerate(peers):
        start = pl.multiple_of((at ^ (place + 1)) * share, share)
        copies.append(start_copy(sent.at[pl.ds(start, share), :], peer, sems.at[2 + place]))
    mine = pl.ds(pl.multiple_of(at * share, share), share)
    kept[...] = part[mine, :]
    kept_norm[...] = norm[mine, :]
    goal_copy.wait()

    def hits(goal):
        shard = 1 + lax.broadcasted_iota(jnp.int32, goal.shape, 1)
        return jnp.where(goal.astype(F32) == shard.astype(F32), 1.0, 0.0)

    counts = jnp.sum(hits(goals[...]), axis=0, keepdims=True)
    row = where[2] * scored.shape[0] + at * share
    own = goals[pl.ds(pl.multiple_of(row, share), share), :]
    kept_count[...] = jnp.maximum(jnp.sum(hits(own) * counts, axis=1, keepdims=True), 1.0)
    for copy in copies:
        copy.wait()


def value_kernel(features, block, count, where, kept, norm, shard_count, *refs):
    got, pieces, crossed = refs[:count], refs[count:-1], refs[-1]
    total, squares = kept[...], norm[...]
    inner = total.shape[1] // 2
    for one in got:
        total = total + one[:, : 2 * inner].astype(F32)
        squares = squares + from_side(one[:, 2 * inner :])
    inverse = lax.rsqrt(squares / features + EPSILON)
    values = (total[:, :inner] * inverse).astype(BF)
    side = side_of(inverse, shard_count[...])
    crossed[...] = total[:, inner:].astype(BF)
    for away, piece in enumerate(pieces):
        if len(pieces) == 1:
            cross = crossed[...]
        else:
            cross = crossed[:, pl.ds(pl.multiple_of((where[0] ^ away) * block, block), block)]
        reach = inner + cross.shape[1]
        piece[:, :inner] = values
        piece[:, inner:reach] = cross
        piece[:, reach:] = side


def gradient_kernel(share, peers, aways, spots, other, where, *refs):
    count = peers * (1 + max(group for group, _ in spots))
    sources, refs = refs[:count], refs[count:]
    every_row, every_scored, lout_in, gram_in, grad_value, grad_out = refs[:6]
    tokens, x, slopes, normed, back, lout, gram, sems = refs[6:]
    first, dp_at, mp_at = where[0] == 1, where[1], where[2]
    take_row = jnp.logical_not(first) if other else first
    keep = share * peers
    width, inner, block = x.shape[1], lout.shape[0], gram.shape[1]
    piece = inner + block + SIDE
    copies = []

    def begin(source, target):
        copies.append(start_copy(source, target, sems.at[len(copies)]))

    ready = []
    for number, (away, (group, place)) in enumerate(zip(aways, spots)):
        start = number * keep
        here = pl.ds(pl.multiple_of((dp_at ^ away) * keep, keep), keep)
        target, sem = x.at[pl.ds(start, keep), :], sems.at[len(copies)]
        scored = every_scored.at[here, :]
        fetch(take_row, every_row.at[here, pl.ds(0, width)], scored, target, sem)
        copies.append(pltpu.make_async_copy(scored, target, sem))
        for mask in range(peers):
            at = pl.multiple_of(start + (mp_at ^ mask) * share, share)
            source = sources[group * peers + mask].at[:, pl.ds(place * piece, piece)]
            begin(source, tokens.at[pl.ds(at, share), :])
        ready.append(len(copies))
        if number == min(1, len(aways) - 1):
            maps = len(copies)
            begin(gram_in, gram)
            begin(lout_in, lout)
    done, step = 0, 2 if len(aways) % 2 == 0 else 1
    for number in range(0, len(aways), step):
        until = ready[number + step - 1]
        for index in range(done, until):
            if index not in (maps, maps + 1):
                copies[index].wait()
        done = until
        here = pl.ds(keep * number, keep * step)
        wide = x[here, :].astype(F32)
        side = tokens[here, inner + block :]
        portion = 1.0 / from_side(side, 1)
        normed[here, :] = (wide * from_side(side)).astype(BF)
        values = tokens[here, :inner]
        crossed = tokens[here, inner : inner + block].astype(F32)
        if number == 0:
            copies[maps].wait()
        back[here, :] = ((crossed + matmul(values, gram[...])) * portion).astype(BF)
        if number == 0:
            copies[maps + 1].wait()
        slopes[here, :] = ((wide + matmul(values, lout[...])) * portion).astype(BF)
    column = pl.ds(pl.multiple_of(dp_at * block, block), block)
    grad_value[...] = matmul_tn(back[...], normed[...]).astype(grad_value.dtype)
    grad_out[...] = matmul_tn(tokens[:, column], slopes[...]).astype(grad_out.dtype)


def add_kernel(value_near, out_near, value_far, out_far, grad_value, grad_out):
    grad_value[...] = value_near[...] + value_far[...].astype(F32)
    grad_out[...] = out_near[...] + out_far[...].astype(F32)


def square_sum(value):
    wide = value.astype(F32)
    return jnp.sum(wide * wide, axis=1, keepdims=True)


def exchange(first, second, first_mask, second_mask):
    first, second = lax.optimization_barrier((first, second))
    return lax.optimization_barrier(
        (flip(first, "mp", first_mask), flip(second, "mp", second_mask))
    )


def on_device(
    candidates,
    scorer_value,
    scorer_out,
    learner_value,
    learner_out,
    keep_index,
    keep_dest,
    keep_count,
):
    first = lax.axis_index("segment") == 0
    dp_at = lax.axis_index("dp")
    mp_at = lax.axis_index("mp")
    dp_size = lax.axis_size("dp")
    mp_size = lax.axis_size("mp")
    keep = keep_index.shape[1]
    width = candidates.shape[1]
    scorer_width = width * mp_size
    learner_width = 2 * scorer_width
    inner = learner_value.shape[2]
    block = inner // dp_size
    share = keep // mp_size

    own_value, own_out = scorer_value[0], scorer_out[0]
    own_lvalue, own_lout = learner_value[0], learner_out[0]
    other_value = flip(own_value, "segment", 1)

    is_live = jnp.arange(keep) < keep_count[0]
    pick = (keep_index[0][:, None] == jnp.arange(candidates.shape[0])[None, :]) & is_live[:, None]
    rows = matmul(pick.astype(BF), candidates).astype(BF)
    goal = jnp.where(is_live, keep_dest[0] + 1, 0).astype(F32)[:, None]
    rows_wide = jnp.concatenate([rows, jnp.broadcast_to(goal, (keep, SIDE)).astype(BF)], axis=1)

    def repeat(array):
        return call(
            repeat_kernel,
            [pltpu.HBM((dp_size * keep, array.shape[1]), BF)],
            [VMEM],
            [pltpu.SemaphoreType.DMA((dp_size,))],
            out_specs=[HBM],
        )(array)[0]

    gram = matmul_nt(own_lout, lax.dynamic_slice_in_dim(own_lout, dp_at * block, block, 0))
    half = inner // 2
    at = lax.axis_index("segment")
    kept_half = lax.dynamic_slice_in_dim(gram, at * half, half, 0)
    sent_half = lax.dynamic_slice_in_dim(gram, (1 - at) * half, half, 0)
    got_half = flip(sent_half.astype(BF), "segment", 1)

    direct = dp_size <= 8 and block % SIDE == 0
    flag = first.astype(jnp.int32)
    half_rows = keep // 2
    sums = [jax.ShapeDtypeStruct((keep, inner), F32), jax.ShapeDtypeStruct((keep, 1), F32)]
    state = sums + [jax.ShapeDtypeStruct((half_rows, inner + SIDE), BF)] * 2
    wide_state = state
    if direct:
        extra = half * block // keep
        wide_state = sums + [jax.ShapeDtypeStruct((half_rows, inner + SIDE + extra), BF)] * 2
        wide_state.append(jax.ShapeDtypeStruct((half, block), F32))
    hidden_type = jax.ShapeDtypeStruct((keep, width), BF)
    where = jnp.stack([flag, mp_at, dp_at])
    weight = pltpu.VMEM(own_value.shape, BF)

    def placed(*arrays):
        return [pltpu.with_memory_space_constraint(array, pltpu.HBM) for array in arrays]

    def halves(outs):
        return outs[0], outs[1], outs[2:4], list(outs[4:])

    outs = call(
        functools.partial(start_kernel, direct),
        wide_state,
        [SMEM, VMEM, HBM, HBM] + [VMEM] * (2 * direct),
        [weight, pltpu.SemaphoreType.DMA],
        mebibytes=12,
    )(where, rows, *placed(own_value, other_value), *((kept_half, got_half) if direct else ()))
    part, rows_squares, sents, gram_sum = halves(outs)
    every_row = lax.all_to_all(repeat(rows_wide), "dp", 0, 0, tiled=True)
    own_out, own_lvalue, own_lout, sents = lax.optimization_barrier(
        (own_out, own_lvalue, own_lout, sents)
    )
    other_out = flip(own_out, "segment", 1)
    other_lvalue = flip(own_lvalue, "segment", 1)
    other_lout = flip(own_lout, "segment", 1)
    got = exchange(*sents, 1, 2)
    outs = call(
        functools.partial(between_kernel, direct), wide_state, [VMEM] * (4 + direct), mebibytes=8
    )(part, rows_squares, *got, *gram_sum)
    part, norm, sents, gram_sum = halves(outs)
    got = exchange(*sents, 2, 1)
    outs = call(
        functools.partial(section_kernel, scorer_width, direct),
        [hidden_type] + state + [jax.ShapeDtypeStruct((half, block), BF)] * direct,
        [SMEM] + [VMEM] * 5 + [HBM] * 4 + [VMEM] * direct,
        [weight, weight, pltpu.SemaphoreType.DMA((2,))],
        mebibytes=12,
    )(where, part, norm, *got, rows, *placed(own_out, other_out, own_value, other_value), *gram_sum)
    middle, outs = outs[0], outs[1:]
    part, norm, sents, gram_sum = halves(outs)
    learner_weights = placed(own_lvalue, other_lvalue, own_lout, other_lout)
    given = call(
        learn_kernel,
        [jax.ShapeDtypeStruct((keep, 2 * inner), F32)],
        [SMEM, VMEM] + [HBM] * 4,
        [weight, weight, pltpu.SemaphoreType.DMA((2,))],
        mebibytes=10,
    )(where, rows, *learner_weights)[0]
    got = exchange(*sents, 1, 2)
    outs = call(functools.partial(between_kernel, False), state, [VMEM] * 4)(part, norm, *got)
    part, norm, sents, _ = halves(outs)
    sents, given = lax.optimization_barrier((sents, given))
    got = exchange(*sents, 2, 1)

    long = 2 * inner + SIDE
    scored, norm, repeated = call(
        functools.partial(score_kernel, scorer_width),
        [hidden_type, sums[1], pltpu.HBM((dp_size * keep, width), BF)],
        [SMEM] + [VMEM] * 6 + [HBM] * 2,
        [weight, pltpu.SemaphoreType.DMA((dp_size + 1,))],
        mebibytes=10,
        out_specs=[VMEM, VMEM, HBM],
    )(
        where,
        part,
        norm,
        *got,
        middle,
        rows_squares,
        *placed(own_out, other_out),
    )
    every_scored = lax.all_to_all(repeated, "dp", 0, 0, tiled=True)
    outs = call(
        functools.partial(share_kernel, share),
        [
            jax.ShapeDtypeStruct((share, 2 * inner), F32),
            jax.ShapeDtypeStruct((share, 1), F32),
            jax.ShapeDtypeStruct((share, 1), F32),
        ]
        + [pltpu.HBM((share, long), BF)] * (mp_size - 1),
        [SMEM] + [VMEM] * 3 + [HBM] * 5,
        [
            weight,
            weight,
            pltpu.VMEM((keep, 2 * inner), F32),
            pltpu.VMEM((keep, long), BF),
            pltpu.VMEM((dp_size * keep, SIDE), BF),
            pltpu.SemaphoreType.DMA((mp_size + 2,)),
        ],
        mebibytes=12,
        out_specs=[VMEM] * 3 + [HBM] * (mp_size - 1),
    )(where, scored, norm, given, *learner_weights, every_row)
    kept, kept_norm, shard_count = outs[:3]

    got = lax.optimization_barrier(
        tuple(flip(peer, "mp", mask) for mask, peer in enumerate(outs[3:], 1))
    )
    pieces = call(
        functools.partial(value_kernel, learner_width, block, mp_size - 1),
        [jax.ShapeDtypeStruct((share, inner + block + SIDE), BF)] * dp_size
        if direct
        else [jax.ShapeDtypeStruct((share, long), BF)],
        [SMEM] + [VMEM] * (mp_size + 2),
        [pltpu.VMEM((share, inner), BF)],
    )(jnp.stack([dp_at]), kept, kept_norm, shard_count, *got)

    if direct:
        gram_half = gram_sum[0]
    else:
        gram_half = lax.psum(kept_half + got_half.astype(F32), "mp").astype(BF)
    gram_other = flip(gram_half, "segment", 1)
    gram = jnp.where(
        first,
        jnp.concatenate([gram_half, gram_other], axis=0),
        jnp.concatenate([gram_other, gram_half], axis=0),
    )

    column = dp_at * block

    def spread(piece):
        whole = jnp.zeros((keep, piece.shape[1]), BF)
        for mask in range(mp_size):
            got = flip(piece, "mp", mask) if mask else piece
            whole = lax.dynamic_update_slice(whole, got, ((mp_at ^ mask) * share, 0))
        return whole

    def add(grads, tokens, place):
        v = tokens[:, :inner]
        xo = tokens[:, inner : inner + block].astype(F32)
        inv = unpack(tokens[:, inner + block :], 0)
        share_count = 1.0 / unpack(tokens[:, inner + block :], 1)
        back = ((xo + matmul(v, gram)) * share_count).astype(BF)
        v_block = lax.dynamic_slice_in_dim(v, column, block, 1)
        row = lax.dynamic_slice(every_row, (place * keep, 0), (keep, width))
        score = lax.dynamic_slice_in_dim(every_scored, place * keep, keep, 0)
        added = []
        for x, lout in (
            (jnp.where(first, row, score), own_lout),
            (jnp.where(first, score, row), other_lout),
        ):
            x = x.astype(F32)
            slopes = ((x + matmul(v, lout)) * share_count).astype(BF)
            normed = (x * inv).astype(BF)
            added += [matmul_tn(back, normed), matmul_tn(v_block, slopes)]
        return [grad + new for grad, new in zip(grads, added)]

    if direct:
        moved = [flip(pieces[away], "dp", away) for away in range(1, dp_size)]
        soon = min(3, mp_size)
        own = [pieces[0]] + [flip(pieces[0], "mp", mask) for mask in range(1, soon)]
        moved, own, diagonal = lax.optimization_barrier((moved, own, pieces[0]))
        own += [flip(diagonal, "mp", mask) for mask in range(soon, mp_size)]
        rest = jnp.concatenate(moved, axis=1) if moved else None
        places_at = jnp.stack([flag, dp_at, mp_at])

        def gradients(aways, spots, groups, inputs, other, kind):
            tokens = len(aways) * keep
            return call(
                functools.partial(gradient_kernel, share, mp_size, aways, spots, other),
                [jax.ShapeDtypeStruct((block, width), kind)] * 2,
                [SMEM] + [HBM] * (len(groups) + 4),
                [
                    pltpu.VMEM((tokens, inner + block + SIDE), BF),
                    pltpu.VMEM((tokens, width), BF),
                    pltpu.VMEM((tokens, width), BF),
                    pltpu.VMEM((tokens, width), BF),
                    pltpu.VMEM((tokens, block), BF),
                    pltpu.VMEM(own_lout.shape, BF),
                    pltpu.VMEM(gram.shape, BF),
                    pltpu.SemaphoreType.DMA((len(aways) * (mp_size + 1) + 2,)),
                ],
                mebibytes=16,
            )(places_at, *groups, *placed(*inputs, other_lout if other else own_lout, gram))

        groups, spots = own, ((0, 0),)
        if dp_size > 1:
            groups = own + [rest] + [flip(rest, "mp", mask) for mask in range(1, mp_size)]
            spots += tuple((1, place) for place in range(dp_size - 1))
        inputs = (every_row, every_scored)
        aways = tuple(range(dp_size))
        far = gradients(aways, spots, groups, inputs, True, BF)
        near = gradients(aways, spots, groups, inputs, False, F32)
    else:
        ring = [(source, (source + 1) % dp_size) for source in range(dp_size)]

        def turn(step, carry):
            grads, full = carry
            cross = lax.dynamic_slice_in_dim(full, inner + column, block, 1)
            piece = jnp.concatenate([full[:, :inner], cross, full[:, 2 * inner :]], axis=1)
            grads = add(grads, spread(piece), (dp_at - step) % dp_size)
            return grads, lax.ppermute(full, "dp", ring)

        grads = [jnp.zeros((block, width), F32)] * 4
        grads, _ = lax.fori_loop(0, dp_size, turn, (grads, pieces[0]))
        near, far = grads[:2], [grad.astype(BF) for grad in grads[2:]]
    got = [flip(sent, "segment", 1) for sent in far]
    grads = call(
        add_kernel,
        [jax.ShapeDtypeStruct((block, width), F32)] * 2,
        [VMEM] * 4,
        mebibytes=10,
    )(*near, *got)
    return (grads[0][None], grads[1][None])


def solution(mesh):
    placed = (
        P(("segment", "dp"), "mp"),
        P("segment", "mp", None),
        P("segment", None, "mp"),
        P("segment", "mp", None),
        P("segment", None, "mp"),
        P(("segment", "dp"), None),
        P(("segment", "dp"), None),
        P(("segment", "dp")),
    )
    return jax.shard_map(
        on_device,
        mesh=mesh,
        in_specs=placed,
        out_specs=(P("segment", "dp", "mp"), P("segment", "dp", "mp")),
        check_vma=False,
    )
```

```python
import functools

import jax
import jax.numpy as jnp
from jax import lax
from jax.experimental import pallas as pl
from jax.experimental.pallas import tpu as pltpu
from jax.sharding import PartitionSpec as P

EPSILON = 1e-05
BF = jnp.bfloat16
F32 = jnp.float32
SIDE = 128


def flip(value, axis, mask):
    pairs = [(source, source ^ mask) for source in range(lax.axis_size(axis))]
    return lax.ppermute(value, axis, pairs)


def matmul(left, right):
    return jnp.dot(left, right, preferred_element_type=F32)


def matmul_nt(left, right):
    return lax.dot_general(left, right, (((1,), (1,)), ((), ())), preferred_element_type=F32)


def matmul_tn(left, right):
    return lax.dot_general(left, right, (((0,), (0,)), ((), ())), preferred_element_type=F32)


def unpack(side, place):
    wide = side[:, 3 * place : 3 * place + 3].astype(F32)
    return wide[:, 0:1] + wide[:, 1:2] + wide[:, 2:3]


VMEM = pl.BlockSpec(memory_space=pltpu.VMEM)
SMEM = pl.BlockSpec(memory_space=pltpu.SMEM)
HBM = pl.BlockSpec(memory_space=pltpu.HBM)


def call(body, outs, in_specs, scratch=(), mebibytes=12, out_specs=None, cost=None):
    return pl.pallas_call(
        body,
        out_shape=outs,
        in_specs=in_specs,
        out_specs=out_specs or [VMEM] * len(outs),
        scratch_shapes=list(scratch),
        compiler_params=pltpu.CompilerParams(vmem_limit_bytes=mebibytes << 20),
        cost_estimate=cost,
    )


def fetch(take_left, left, right, target, sem):
    @pl.when(take_left)
    def _():
        pltpu.make_async_copy(left, target, sem).start()

    @pl.when(jnp.logical_not(take_left))
    def _():
        pltpu.make_async_copy(right, target, sem).start()


def start_copy(source, target, sem):
    copy = pltpu.make_async_copy(source, target, sem)
    copy.start()
    return copy


def side_of(*columns):
    lane = lax.broadcasted_iota(jnp.int32, (columns[0].shape[0], SIDE), 1)
    picked = jnp.zeros(lane.shape, F32)
    for place, column in enumerate(columns):
        high = column.astype(BF).astype(F32)
        middle = (column - high).astype(BF).astype(F32)
        for part, piece in enumerate((high, middle, column - high - middle)):
            picked = jnp.where(lane == 3 * place + part, piece, picked)
    return picked.astype(BF)


def from_side(side, place=0):
    lane = lax.broadcasted_iota(jnp.int32, side.shape, 1)
    own = (lane >= 3 * place) & (lane < 3 * place + 3)
    return jnp.sum(jnp.where(own, side.astype(F32), 0.0), axis=1, keepdims=True)


def emit(part, norm, sents, gram=None):
    half, width = sents[0].shape[0], part.shape[1]
    for place, sent in enumerate(sents):
        start = place * half
        sent[:, :width] = part[start : start + half, :].astype(BF)
        sent[:, width : width + SIDE] = side_of(norm[start : start + half, :])
        if gram is not None:
            for rows, columns in gram_blocks(gram, place, half, width):
                sent[:, columns] = gram[rows, :].astype(BF)


def gram_blocks(gram, place, half, width):
    count, block = gram.shape[0] // 2 // half, gram.shape[1]
    for index in range(count):
        row = (place * count + index) * half
        column = width + SIDE + index * block
        yield slice(row, row + half), slice(column, column + block)


def absorb(part, norm, gots, gram=None, gram_sum=None):
    half, width = gots[0].shape[0], part.shape[1]
    parts, norms = [], []
    for place, got in enumerate(gots):
        start = place * half
        parts.append(part[start : start + half, :] + got[:, :width].astype(F32))
        side = got[:, width : width + SIDE]
        norms.append(norm[start : start + half, :] + from_side(side))
        if gram is not None:
            for rows, columns in gram_blocks(gram, place, half, width):
                summed = gram[rows, :] + got[:, columns].astype(F32)
                gram_sum[rows, :] = summed.astype(gram_sum.dtype)
    return jnp.concatenate(parts, axis=0), jnp.concatenate(norms, axis=0)


def start_kernel(with_gram, where, rows, value_a, value_b, *refs):
    gram_a, gram_b = refs[:2] if with_gram else (None, None)
    refs = refs[2:] if with_gram else refs
    part, norm, top, low = refs[:4]
    gram, (repeated, weight, sem, sems) = refs[4] if with_gram else None, refs[-4:]
    fetch(where[0] == 1, value_a, value_b, weight, sem)
    keep = rows.shape[0]
    copies = [
        start_copy(rows, repeated.at[pl.ds(place * keep, keep), :], sems.at[place])
        for place in range(repeated.shape[0] // keep)
    ]
    row = rows[:, : weight.shape[0]]
    norm[...] = square_sum(row)
    if with_gram:
        gram[...] = gram_a[...] + gram_b[...].astype(F32)
    pltpu.make_async_copy(value_a, weight, sem).wait()
    part[...] = matmul(row, weight[...])
    emit(part, norm, (top, low), gram)
    for copy in copies:
        copy.wait()


def between_kernel(with_gram, part_in, norm_in, got_top, got_low, *refs):
    gram_in, refs = (refs[0], refs[1:]) if with_gram else (None, refs)
    part, norm, top, low = refs[:4]
    gram = refs[4] if with_gram else None
    part[...], norm[...] = absorb(part_in, norm_in, (got_top, got_low), gram_in, gram)
    emit(part, norm, (top, low), gram)


def section_kernel(features, with_gram, where, *refs):
    part_in, norm_in, got_top, got_low, rows, out_a, out_b, value_a, value_b = refs[:9]
    gram_in, refs = (refs[9], refs[10:]) if with_gram else (None, refs[9:])
    middle, part, norm, top, low = refs[:5]
    gram, (out, value, sems) = refs[5] if with_gram else None, refs[-3:]
    first = where[0] == 1
    fetch(first, out_a, out_b, out, sems.at[0])
    fetch(first, value_b, value_a, value, sems.at[1])
    total, squares = absorb(part_in, norm_in, (got_top, got_low), gram_in, gram)
    values = (total * lax.rsqrt(squares / features + EPSILON)).astype(BF)
    pltpu.make_async_copy(out_a, out, sems.at[0]).wait()
    hidden = (rows[...].astype(F32) + matmul(values, out[...])).astype(BF)
    middle[...] = hidden
    norm[...] = square_sum(hidden)
    pltpu.make_async_copy(value_a, value, sems.at[1]).wait()
    part[...] = matmul(hidden, value[...])
    emit(part, norm, (top, low))


def learn_kernel(where, rows, value_a, value_b, lout_a, lout_b, part, value, lout, sems):
    first = where[0] == 1
    fetch(first, value_a, value_b, value, sems.at[0])
    fetch(first, lout_a, lout_b, lout, sems.at[1])
    inner = value.shape[1]
    pltpu.make_async_copy(value_a, value, sems.at[0]).wait()
    part[:, :inner] = matmul(rows[...], value[...])
    pltpu.make_async_copy(lout_a, lout, sems.at[1]).wait()
    part[:, inner:] = matmul_nt(rows[...], lout[...])


def score_kernel(features, where, *refs):
    part_in, norm_in, got_top, got_low, middle, rows_squares, out_a, out_b = refs[:8]
    scored, norm, repeated, out, sems = refs[8:]
    fetch(where[0] == 1, out_b, out_a, out, sems.at[0])
    total, squares = absorb(part_in, norm_in, (got_top, got_low))
    values = (total * lax.rsqrt(squares / features + EPSILON)).astype(BF)
    pltpu.make_async_copy(out_a, out, sems.at[0]).wait()
    score = (middle[...].astype(F32) + matmul(values, out[...])).astype(BF)
    scored[...] = score
    keep = score.shape[0]
    copies = [
        start_copy(scored, repeated.at[pl.ds(place * keep, keep), :], sems.at[1 + place])
        for place in range(repeated.shape[0] // keep)
    ]
    norm[...] = rows_squares[...] + square_sum(score)
    for copy in copies:
        copy.wait()


def share_kernel(share, where, scored, norm, given, value_a, value_b, lout_a, lout_b, *refs):
    every_row, kept, kept_norm, kept_count = refs[:4]
    peers, (value, lout, part, sent, goals, sems) = refs[4:-6], refs[-6:]
    sides = every_row.at[:, pl.ds(scored.shape[1], SIDE)]
    goal_copy = start_copy(sides, goals, sems.at[sems.shape[0] - 1])
    first, at = where[0] == 1, where[1]
    fetch(first, value_b, value_a, value, sems.at[0])
    fetch(first, lout_b, lout_a, lout, sems.at[1])
    inner = value.shape[1]
    score = scored[...]
    sent[:, 2 * inner :] = side_of(norm[...])
    pltpu.make_async_copy(value_a, value, sems.at[0]).wait()
    part[:, :inner] = given[:, :inner] + matmul(score, value[...])
    sent[:, :inner] = part[:, :inner].astype(BF)
    pltpu.make_async_copy(lout_a, lout, sems.at[1]).wait()
    part[:, inner:] = given[:, inner:] + matmul_nt(score, lout[...])
    sent[:, inner : 2 * inner] = part[:, inner:].astype(BF)
    copies = []
    for place, peer in enumerate(peers):
        start = pl.multiple_of((at ^ (place + 1)) * share, share)
        copies.append(start_copy(sent.at[pl.ds(start, share), :], peer, sems.at[2 + place]))
    mine = pl.ds(pl.multiple_of(at * share, share), share)
    kept[...] = part[mine, :]
    kept_norm[...] = norm[mine, :]
    goal_copy.wait()

    def hits(goal):
        shard = 1 + lax.broadcasted_iota(jnp.int32, goal.shape, 1)
        return jnp.where(goal.astype(F32) == shard.astype(F32), 1.0, 0.0)

    counts = jnp.sum(hits(goals[...]), axis=0, keepdims=True)
    row = where[2] * scored.shape[0] + at * share
    own = goals[pl.ds(pl.multiple_of(row, share), share), :]
    kept_count[...] = jnp.maximum(jnp.sum(hits(own) * counts, axis=1, keepdims=True), 1.0)
    for copy in copies:
        copy.wait()


def value_kernel(features, block, count, where, kept, norm, shard_count, *refs):
    got, pieces, crossed = refs[:count], refs[count:-1], refs[-1]
    total, squares = kept[...], norm[...]
    inner = total.shape[1] // 2
    for one in got:
        total = total + one[:, : 2 * inner].astype(F32)
        squares = squares + from_side(one[:, 2 * inner :])
    inverse = lax.rsqrt(squares / features + EPSILON)
    values = (total[:, :inner] * inverse).astype(BF)
    side = side_of(inverse, shard_count[...])
    crossed[...] = total[:, inner:].astype(BF)
    for away, piece in enumerate(pieces):
        if len(pieces) == 1:
            cross = crossed[...]
        else:
            cross = crossed[:, pl.ds(pl.multiple_of((where[0] ^ away) * block, block), block)]
        reach = inner + cross.shape[1]
        piece[:, :inner] = values
        piece[:, inner:reach] = cross
        piece[:, reach:] = side


def gradient_kernel(share, peers, aways, spots, other, where, *refs):
    count = peers * (1 + max(group for group, _ in spots))
    sources, refs = refs[:count], refs[count:]
    every_row, every_scored, lout_in, gram_in, grad_value, grad_out = refs[:6]
    tokens, x, slopes, normed, back, lout, gram, sems = refs[6:]
    first, dp_at, mp_at = where[0] == 1, where[1], where[2]
    take_row = jnp.logical_not(first) if other else first
    keep = share * peers
    width, inner, block = x.shape[1], lout.shape[0], gram.shape[1]
    piece = inner + block + SIDE
    copies = []

    def begin(source, target):
        copies.append(start_copy(source, target, sems.at[len(copies)]))

    ready = []
    for number, (away, (group, place)) in enumerate(zip(aways, spots)):
        start = number * keep
        here = pl.ds(pl.multiple_of((dp_at ^ away) * keep, keep), keep)
        target, sem = x.at[pl.ds(start, keep), :], sems.at[len(copies)]
        scored = every_scored.at[here, :]
        fetch(take_row, every_row.at[here, pl.ds(0, width)], scored, target, sem)
        copies.append(pltpu.make_async_copy(scored, target, sem))
        for mask in range(peers):
            at = pl.multiple_of(start + (mp_at ^ mask) * share, share)
            source = sources[group * peers + mask].at[:, pl.ds(place * piece, piece)]
            begin(source, tokens.at[pl.ds(at, share), :])
        ready.append(len(copies))
        if number == min(1, len(aways) - 1):
            maps = len(copies)
            begin(gram_in, gram)
            begin(lout_in, lout)
    done, step = 0, 2 if len(aways) % 2 == 0 else 1
    for number in range(0, len(aways), step):
        until = ready[number + step - 1]
        for index in range(done, until):
            if index not in (maps, maps + 1):
                copies[index].wait()
        done = until
        here = pl.ds(keep * number, keep * step)
        wide = x[here, :].astype(F32)
        side = tokens[here, inner + block :]
        portion = 1.0 / from_side(side, 1)
        normed[here, :] = (wide * from_side(side)).astype(BF)
        values = tokens[here, :inner]
        crossed = tokens[here, inner : inner + block].astype(F32)
        if number == 0:
            copies[maps].wait()
        back[here, :] = ((crossed + matmul(values, gram[...])) * portion).astype(BF)
        if number == 0:
            copies[maps + 1].wait()
        slopes[here, :] = ((wide + matmul(values, lout[...])) * portion).astype(BF)
    column = pl.ds(pl.multiple_of(dp_at * block, block), block)
    grad_value[...] = matmul_tn(back[...], normed[...]).astype(grad_value.dtype)
    grad_out[...] = matmul_tn(tokens[:, column], slopes[...]).astype(grad_out.dtype)


def add_kernel(value_near, out_near, value_far, out_far, grad_value, grad_out):
    grad_value[...] = value_near[...] + value_far[...].astype(F32)
    grad_out[...] = out_near[...] + out_far[...].astype(F32)


def square_sum(value):
    wide = value.astype(F32)
    return jnp.sum(wide * wide, axis=1, keepdims=True)


def exchange(first, second, first_mask, second_mask):
    first, second = lax.optimization_barrier((first, second))
    return lax.optimization_barrier(
        (flip(first, "mp", first_mask), flip(second, "mp", second_mask))
    )


def on_device(
    candidates,
    scorer_value,
    scorer_out,
    learner_value,
    learner_out,
    keep_index,
    keep_dest,
    keep_count,
):
    first = lax.axis_index("segment") == 0
    dp_at = lax.axis_index("dp")
    mp_at = lax.axis_index("mp")
    dp_size = lax.axis_size("dp")
    mp_size = lax.axis_size("mp")
    keep = keep_index.shape[1]
    width = candidates.shape[1]
    scorer_width = width * mp_size
    learner_width = 2 * scorer_width
    inner = learner_value.shape[2]
    block = inner // dp_size
    share = keep // mp_size

    own_value, own_out = scorer_value[0], scorer_out[0]
    own_lvalue, own_lout = learner_value[0], learner_out[0]
    other_value = flip(own_value, "segment", 1)

    is_live = jnp.arange(keep) < keep_count[0]
    pick = (keep_index[0][:, None] == jnp.arange(candidates.shape[0])[None, :]) & is_live[:, None]
    rows = matmul(pick.astype(BF), candidates).astype(BF)
    goal = jnp.where(is_live, keep_dest[0] + 1, 0).astype(F32)[:, None]
    rows_wide = jnp.concatenate([rows, jnp.broadcast_to(goal, (keep, SIDE)).astype(BF)], axis=1)

    gram = matmul_nt(own_lout, lax.dynamic_slice_in_dim(own_lout, dp_at * block, block, 0))
    half = inner // 2
    at = lax.axis_index("segment")
    kept_half = lax.dynamic_slice_in_dim(gram, at * half, half, 0)
    sent_half = lax.dynamic_slice_in_dim(gram, (1 - at) * half, half, 0)
    got_half = flip(sent_half.astype(BF), "segment", 1)

    direct = dp_size <= 8 and block % SIDE == 0
    flag = first.astype(jnp.int32)
    half_rows = keep // 2
    sums = [jax.ShapeDtypeStruct((keep, inner), F32), jax.ShapeDtypeStruct((keep, 1), F32)]
    state = sums + [jax.ShapeDtypeStruct((half_rows, inner + SIDE), BF)] * 2
    wide_state = state
    if direct:
        extra = half * block // keep
        wide_state = sums + [jax.ShapeDtypeStruct((half_rows, inner + SIDE + extra), BF)] * 2
        wide_state.append(jax.ShapeDtypeStruct((half, block), F32))
    hidden_type = jax.ShapeDtypeStruct((keep, width), BF)
    where = jnp.stack([flag, mp_at, dp_at])
    weight = pltpu.VMEM(own_value.shape, BF)

    def placed(*arrays):
        return [pltpu.with_memory_space_constraint(array, pltpu.HBM) for array in arrays]

    def halves(outs):
        return outs[0], outs[1], outs[2:4], list(outs[4:])

    *outs, repeated = call(
        functools.partial(start_kernel, direct),
        wide_state + [pltpu.HBM((dp_size * keep, width + SIDE), BF)],
        [SMEM, VMEM, HBM, HBM] + [VMEM] * (2 * direct),
        [weight, pltpu.SemaphoreType.DMA, pltpu.SemaphoreType.DMA((dp_size,))],
        mebibytes=12,
        out_specs=[VMEM] * len(wide_state) + [HBM],
    )(
        where,
        rows_wide,
        *placed(own_value, other_value),
        *((kept_half, got_half) if direct else ()),
    )
    part, rows_squares, sents, gram_sum = halves(outs)
    every_row = lax.all_to_all(repeated, "dp", 0, 0, tiled=True)
    own_out, own_lvalue, own_lout, sents = lax.optimization_barrier(
        (own_out, own_lvalue, own_lout, sents)
    )
    other_out = flip(own_out, "segment", 1)
    other_lvalue = flip(own_lvalue, "segment", 1)
    other_lout = flip(own_lout, "segment", 1)
    got = exchange(*sents, 1, 2)
    outs = call(
        functools.partial(between_kernel, direct), wide_state, [VMEM] * (4 + direct), mebibytes=8
    )(part, rows_squares, *got, *gram_sum)
    part, norm, sents, gram_sum = halves(outs)
    got = exchange(*sents, 2, 1)
    outs = call(
        functools.partial(section_kernel, scorer_width, direct),
        [hidden_type] + state + [jax.ShapeDtypeStruct((half, block), BF)] * direct,
        [SMEM] + [VMEM] * 5 + [HBM] * 4 + [VMEM] * direct,
        [weight, weight, pltpu.SemaphoreType.DMA((2,))],
        mebibytes=12,
    )(where, part, norm, *got, rows, *placed(own_out, other_out, own_value, other_value), *gram_sum)
    middle, outs = outs[0], outs[1:]
    part, norm, sents, gram_sum = halves(outs)
    learner_weights = placed(own_lvalue, other_lvalue, own_lout, other_lout)
    given = call(
        learn_kernel,
        [jax.ShapeDtypeStruct((keep, 2 * inner), F32)],
        [SMEM, VMEM] + [HBM] * 4,
        [weight, weight, pltpu.SemaphoreType.DMA((2,))],
        mebibytes=10,
    )(where, rows, *learner_weights)[0]
    got = exchange(*sents, 1, 2)
    outs = call(functools.partial(between_kernel, False), state, [VMEM] * 4)(part, norm, *got)
    part, norm, sents, _ = halves(outs)
    sents, given = lax.optimization_barrier((sents, given))
    got = exchange(*sents, 2, 1)

    long = 2 * inner + SIDE
    scored, norm, repeated = call(
        functools.partial(score_kernel, scorer_width),
        [hidden_type, sums[1], pltpu.HBM((dp_size * keep, width), BF)],
        [SMEM] + [VMEM] * 6 + [HBM] * 2,
        [weight, pltpu.SemaphoreType.DMA((dp_size + 1,))],
        mebibytes=10,
        out_specs=[VMEM, VMEM, HBM],
    )(
        where,
        part,
        norm,
        *got,
        middle,
        rows_squares,
        *placed(own_out, other_out),
    )
    every_scored = lax.all_to_all(repeated, "dp", 0, 0, tiled=True)
    outs = call(
        functools.partial(share_kernel, share),
        [
            jax.ShapeDtypeStruct((share, 2 * inner), F32),
            jax.ShapeDtypeStruct((share, 1), F32),
            jax.ShapeDtypeStruct((share, 1), F32),
        ]
        + [pltpu.HBM((share, long), BF)] * (mp_size - 1),
        [SMEM] + [VMEM] * 3 + [HBM] * 5,
        [
            weight,
            weight,
            pltpu.VMEM((keep, 2 * inner), F32),
            pltpu.VMEM((keep, long), BF),
            pltpu.VMEM((dp_size * keep, SIDE), BF),
            pltpu.SemaphoreType.DMA((mp_size + 2,)),
        ],
        mebibytes=12,
        out_specs=[VMEM] * 3 + [HBM] * (mp_size - 1),
    )(where, scored, norm, given, *learner_weights, every_row)
    kept, kept_norm, shard_count = outs[:3]

    got = lax.optimization_barrier(
        tuple(flip(peer, "mp", mask) for mask, peer in enumerate(outs[3:], 1))
    )
    pieces = call(
        functools.partial(value_kernel, learner_width, block, mp_size - 1),
        [jax.ShapeDtypeStruct((share, inner + block + SIDE), BF)] * dp_size
        if direct
        else [jax.ShapeDtypeStruct((share, long), BF)],
        [SMEM] + [VMEM] * (mp_size + 2),
        [pltpu.VMEM((share, inner), BF)],
    )(jnp.stack([dp_at]), kept, kept_norm, shard_count, *got)

    if direct:
        gram_half = gram_sum[0]
    else:
        gram_half = lax.psum(kept_half + got_half.astype(F32), "mp").astype(BF)
    gram_other = flip(gram_half, "segment", 1)
    gram = jnp.where(
        first,
        jnp.concatenate([gram_half, gram_other], axis=0),
        jnp.concatenate([gram_other, gram_half], axis=0),
    )

    column = dp_at * block

    def spread(piece):
        whole = jnp.zeros((keep, piece.shape[1]), BF)
        for mask in range(mp_size):
            got = flip(piece, "mp", mask) if mask else piece
            whole = lax.dynamic_update_slice(whole, got, ((mp_at ^ mask) * share, 0))
        return whole

    def add(grads, tokens, place):
        v = tokens[:, :inner]
        xo = tokens[:, inner : inner + block].astype(F32)
        inv = unpack(tokens[:, inner + block :], 0)
        share_count = 1.0 / unpack(tokens[:, inner + block :], 1)
        back = ((xo + matmul(v, gram)) * share_count).astype(BF)
        v_block = lax.dynamic_slice_in_dim(v, column, block, 1)
        row = lax.dynamic_slice(every_row, (place * keep, 0), (keep, width))
        score = lax.dynamic_slice_in_dim(every_scored, place * keep, keep, 0)
        added = []
        for x, lout in (
            (jnp.where(first, row, score), own_lout),
            (jnp.where(first, score, row), other_lout),
        ):
            x = x.astype(F32)
            slopes = ((x + matmul(v, lout)) * share_count).astype(BF)
            normed = (x * inv).astype(BF)
            added += [matmul_tn(back, normed), matmul_tn(v_block, slopes)]
        return [grad + new for grad, new in zip(grads, added)]

    if direct:
        moved = [flip(pieces[away], "dp", away) for away in range(1, dp_size)]
        soon = min(3, mp_size)
        own = [pieces[0]] + [flip(pieces[0], "mp", mask) for mask in range(1, soon)]
        moved, own, diagonal = lax.optimization_barrier((moved, own, pieces[0]))
        own += [flip(diagonal, "mp", mask) for mask in range(soon, mp_size)]
        rest = jnp.concatenate(moved, axis=1) if moved else None
        places_at = jnp.stack([flag, dp_at, mp_at])

        def gradients(aways, spots, groups, inputs, other, kind):
            tokens = len(aways) * keep
            return call(
                functools.partial(gradient_kernel, share, mp_size, aways, spots, other),
                [jax.ShapeDtypeStruct((block, width), kind)] * 2,
                [SMEM] + [HBM] * (len(groups) + 4),
                [
                    pltpu.VMEM((tokens, inner + block + SIDE), BF),
                    pltpu.VMEM((tokens, width), BF),
                    pltpu.VMEM((tokens, width), BF),
                    pltpu.VMEM((tokens, width), BF),
                    pltpu.VMEM((tokens, block), BF),
                    pltpu.VMEM(own_lout.shape, BF),
                    pltpu.VMEM(gram.shape, BF),
                    pltpu.SemaphoreType.DMA((len(aways) * (mp_size + 1) + 2,)),
                ],
                mebibytes=16,
            )(places_at, *groups, *placed(*inputs, other_lout if other else own_lout, gram))

        groups, spots = own, ((0, 0),)
        if dp_size > 1:
            groups = own + [rest] + [flip(rest, "mp", mask) for mask in range(1, mp_size)]
            spots += tuple((1, place) for place in range(dp_size - 1))
        inputs = (every_row, every_scored)
        aways = tuple(range(dp_size))
        far = gradients(aways, spots, groups, inputs, True, BF)
        near = gradients(aways, spots, groups, inputs, False, F32)
    else:
        ring = [(source, (source + 1) % dp_size) for source in range(dp_size)]

        def turn(step, carry):
            grads, full = carry
            cross = lax.dynamic_slice_in_dim(full, inner + column, block, 1)
            piece = jnp.concatenate([full[:, :inner], cross, full[:, 2 * inner :]], axis=1)
            grads = add(grads, spread(piece), (dp_at - step) % dp_size)
            return grads, lax.ppermute(full, "dp", ring)

        grads = [jnp.zeros((block, width), F32)] * 4
        grads, _ = lax.fori_loop(0, dp_size, turn, (grads, pieces[0]))
        near, far = grads[:2], [grad.astype(BF) for grad in grads[2:]]
    got = [flip(sent, "segment", 1) for sent in far]
    grads = call(
        add_kernel,
        [jax.ShapeDtypeStruct((block, width), F32)] * 2,
        [VMEM] * 4,
        mebibytes=10,
    )(*near, *got)
    return (grads[0][None], grads[1][None])


def solution(mesh):
    placed = (
        P(("segment", "dp"), "mp"),
        P("segment", "mp", None),
        P("segment", None, "mp"),
        P("segment", "mp", None),
        P("segment", None, "mp"),
        P(("segment", "dp"), None),
        P(("segment", "dp"), None),
        P(("segment", "dp")),
    )
    return jax.shard_map(
        on_device,
        mesh=mesh,
        in_specs=placed,
        out_specs=(P("segment", "dp", "mp"), P("segment", "dp", "mp")),
        check_vma=False,
    )
```

```python
import functools

import jax
import jax.numpy as jnp
from jax import lax
from jax.experimental import pallas as pl
from jax.experimental.pallas import tpu as pltpu
from jax.sharding import PartitionSpec as P

EPSILON = 1e-05
BF = jnp.bfloat16
F32 = jnp.float32
SIDE = 128


def flip(value, axis, mask):
    pairs = [(source, source ^ mask) for source in range(lax.axis_size(axis))]
    return lax.ppermute(value, axis, pairs)


def matmul(left, right):
    return jnp.dot(left, right, preferred_element_type=F32)


def matmul_nt(left, right):
    return lax.dot_general(left, right, (((1,), (1,)), ((), ())), preferred_element_type=F32)


def matmul_tn(left, right):
    return lax.dot_general(left, right, (((0,), (0,)), ((), ())), preferred_element_type=F32)


def unpack(side, place):
    wide = side[:, 3 * place : 3 * place + 3].astype(F32)
    return wide[:, 0:1] + wide[:, 1:2] + wide[:, 2:3]


VMEM = pl.BlockSpec(memory_space=pltpu.VMEM)
SMEM = pl.BlockSpec(memory_space=pltpu.SMEM)
HBM = pl.BlockSpec(memory_space=pltpu.HBM)


def call(body, outs, in_specs, scratch=(), mebibytes=12, out_specs=None, cost=None):
    return pl.pallas_call(
        body,
        out_shape=outs,
        in_specs=in_specs,
        out_specs=out_specs or [VMEM] * len(outs),
        scratch_shapes=list(scratch),
        compiler_params=pltpu.CompilerParams(vmem_limit_bytes=mebibytes << 20),
        cost_estimate=cost,
    )


def fetch(take_left, left, right, target, sem):
    @pl.when(take_left)
    def _():
        pltpu.make_async_copy(left, target, sem).start()

    @pl.when(jnp.logical_not(take_left))
    def _():
        pltpu.make_async_copy(right, target, sem).start()


def start_copy(source, target, sem):
    copy = pltpu.make_async_copy(source, target, sem)
    copy.start()
    return copy


def side_of(*columns):
    lane = lax.broadcasted_iota(jnp.int32, (columns[0].shape[0], SIDE), 1)
    picked = jnp.zeros(lane.shape, F32)
    for place, column in enumerate(columns):
        high = column.astype(BF).astype(F32)
        middle = (column - high).astype(BF).astype(F32)
        for part, piece in enumerate((high, middle, column - high - middle)):
            picked = jnp.where(lane == 3 * place + part, piece, picked)
    return picked.astype(BF)


def from_side(side, place=0):
    lane = lax.broadcasted_iota(jnp.int32, side.shape, 1)
    own = (lane >= 3 * place) & (lane < 3 * place + 3)
    return jnp.sum(jnp.where(own, side.astype(F32), 0.0), axis=1, keepdims=True)


def emit(part, norm, sents, gram=None):
    half, width = sents[0].shape[0], part.shape[1]
    for place, sent in enumerate(sents):
        start = place * half
        sent[:, :width] = part[start : start + half, :].astype(BF)
        sent[:, width : width + SIDE] = side_of(norm[start : start + half, :])
        if gram is not None:
            for rows, columns in gram_blocks(gram, place, half, width):
                sent[:, columns] = gram[rows, :].astype(BF)


def gram_blocks(gram, place, half, width):
    count, block = gram.shape[0] // 2 // half, gram.shape[1]
    for index in range(count):
        row = (place * count + index) * half
        column = width + SIDE + index * block
        yield slice(row, row + half), slice(column, column + block)


def absorb(part, norm, gots, gram=None, gram_sum=None):
    half, width = gots[0].shape[0], part.shape[1]
    parts, norms = [], []
    for place, got in enumerate(gots):
        start = place * half
        parts.append(part[start : start + half, :] + got[:, :width].astype(F32))
        side = got[:, width : width + SIDE]
        norms.append(norm[start : start + half, :] + from_side(side))
        if gram is not None:
            for rows, columns in gram_blocks(gram, place, half, width):
                summed = gram[rows, :] + got[:, columns].astype(F32)
                gram_sum[rows, :] = summed.astype(gram_sum.dtype)
    return jnp.concatenate(parts, axis=0), jnp.concatenate(norms, axis=0)


def start_kernel(with_gram, where, rows, value_a, value_b, *refs):
    gram_a, gram_b = refs[:2] if with_gram else (None, None)
    refs = refs[2:] if with_gram else refs
    part, norm, top, low = refs[:4]
    gram, (repeated, weight, sem, sems) = refs[4] if with_gram else None, refs[-4:]
    fetch(where[0] == 1, value_a, value_b, weight, sem)
    keep = rows.shape[0]
    copies = [
        start_copy(rows, repeated.at[pl.ds(place * keep, keep), :], sems.at[place])
        for place in range(repeated.shape[0] // keep)
    ]
    row = rows[:, : weight.shape[0]]
    norm[...] = square_sum(row)
    if with_gram:
        gram[...] = gram_a[...] + gram_b[...].astype(F32)
    pltpu.make_async_copy(value_a, weight, sem).wait()
    part[...] = matmul(row, weight[...])
    emit(part, norm, (top, low), gram)
    for copy in copies:
        copy.wait()


def between_kernel(with_gram, part_in, norm_in, got_top, got_low, *refs):
    gram_in, refs = (refs[0], refs[1:]) if with_gram else (None, refs)
    part, norm, top, low = refs[:4]
    gram = refs[4] if with_gram else None
    part[...], norm[...] = absorb(part_in, norm_in, (got_top, got_low), gram_in, gram)
    emit(part, norm, (top, low), gram)


def section_kernel(features, with_gram, where, *refs):
    part_in, norm_in, got_top, got_low, rows, out_a, out_b, value_a, value_b = refs[:9]
    gram_in, refs = (refs[9], refs[10:]) if with_gram else (None, refs[9:])
    middle, part, norm, top, low = refs[:5]
    gram, (out, value, sems) = refs[5] if with_gram else None, refs[-3:]
    first = where[0] == 1
    fetch(first, out_a, out_b, out, sems.at[0])
    fetch(first, value_b, value_a, value, sems.at[1])
    total, squares = absorb(part_in, norm_in, (got_top, got_low), gram_in, gram)
    values = (total * lax.rsqrt(squares / features + EPSILON)).astype(BF)
    pltpu.make_async_copy(out_a, out, sems.at[0]).wait()
    hidden = (rows[...].astype(F32) + matmul(values, out[...])).astype(BF)
    middle[...] = hidden
    norm[...] = square_sum(hidden)
    pltpu.make_async_copy(value_a, value, sems.at[1]).wait()
    part[...] = matmul(hidden, value[...])
    emit(part, norm, (top, low))


def learn_kernel(where, rows, value_a, value_b, lout_a, lout_b, part, value, lout, sems):
    first = where[0] == 1
    fetch(first, value_a, value_b, value, sems.at[0])
    fetch(first, lout_a, lout_b, lout, sems.at[1])
    inner = value.shape[1]
    pltpu.make_async_copy(value_a, value, sems.at[0]).wait()
    part[:, :inner] = matmul(rows[...], value[...])
    pltpu.make_async_copy(lout_a, lout, sems.at[1]).wait()
    part[:, inner:] = matmul_nt(rows[...], lout[...])


def score_kernel(features, where, *refs):
    part_in, norm_in, got_top, got_low, middle, rows_squares, out_a, out_b = refs[:8]
    scored, norm, repeated, out, sems = refs[8:]
    fetch(where[0] == 1, out_b, out_a, out, sems.at[0])
    total, squares = absorb(part_in, norm_in, (got_top, got_low))
    values = (total * lax.rsqrt(squares / features + EPSILON)).astype(BF)
    pltpu.make_async_copy(out_a, out, sems.at[0]).wait()
    score = (middle[...].astype(F32) + matmul(values, out[...])).astype(BF)
    scored[...] = score
    keep = score.shape[0]
    copies = [
        start_copy(scored, repeated.at[pl.ds(place * keep, keep), :], sems.at[1 + place])
        for place in range(repeated.shape[0] // keep)
    ]
    norm[...] = rows_squares[...] + square_sum(score)
    for copy in copies:
        copy.wait()


def share_kernel(share, where, scored, norm, given, value_a, value_b, lout_a, lout_b, *refs):
    every_row, kept, kept_norm, kept_count = refs[:4]
    peers, (value, lout, part, sent, goals, sems) = refs[4:-6], refs[-6:]
    first, at = where[0] == 1, where[1]
    fetch(first, value_b, value_a, value, sems.at[0])
    fetch(first, lout_b, lout_a, lout, sems.at[1])
    sides = every_row.at[:, pl.ds(scored.shape[1], SIDE)]
    goal_copy = start_copy(sides, goals, sems.at[sems.shape[0] - 1])
    inner = value.shape[1]
    score = scored[...]
    sent[:, 2 * inner :] = side_of(norm[...])
    pltpu.make_async_copy(value_a, value, sems.at[0]).wait()
    part[:, :inner] = given[:, :inner] + matmul(score, value[...])
    sent[:, :inner] = part[:, :inner].astype(BF)
    pltpu.make_async_copy(lout_a, lout, sems.at[1]).wait()
    part[:, inner:] = given[:, inner:] + matmul_nt(score, lout[...])
    sent[:, inner : 2 * inner] = part[:, inner:].astype(BF)
    copies = []
    for place, peer in enumerate(peers):
        start = pl.multiple_of((at ^ (place + 1)) * share, share)
        copies.append(start_copy(sent.at[pl.ds(start, share), :], peer, sems.at[2 + place]))
    mine = pl.ds(pl.multiple_of(at * share, share), share)
    kept[...] = part[mine, :]
    kept_norm[...] = norm[mine, :]
    goal_copy.wait()

    def hits(goal):
        shard = 1 + lax.broadcasted_iota(jnp.int32, goal.shape, 1)
        return jnp.where(goal.astype(F32) == shard.astype(F32), 1.0, 0.0)

    counts = jnp.sum(hits(goals[...]), axis=0, keepdims=True)
    row = where[2] * scored.shape[0] + at * share
    own = goals[pl.ds(pl.multiple_of(row, share), share), :]
    kept_count[...] = jnp.maximum(jnp.sum(hits(own) * counts, axis=1, keepdims=True), 1.0)
    for copy in copies:
        copy.wait()


def value_kernel(features, block, count, where, kept, norm, shard_count, *refs):
    got, pieces, crossed = refs[:count], refs[count:-1], refs[-1]
    total, squares = kept[...], norm[...]
    inner = total.shape[1] // 2
    for one in got:
        total = total + one[:, : 2 * inner].astype(F32)
        squares = squares + from_side(one[:, 2 * inner :])
    inverse = lax.rsqrt(squares / features + EPSILON)
    values = (total[:, :inner] * inverse).astype(BF)
    side = side_of(inverse, shard_count[...])
    crossed[...] = total[:, inner:].astype(BF)
    for away, piece in enumerate(pieces):
        if len(pieces) == 1:
            cross = crossed[...]
        else:
            cross = crossed[:, pl.ds(pl.multiple_of((where[0] ^ away) * block, block), block)]
        reach = inner + cross.shape[1]
        piece[:, :inner] = values
        piece[:, inner:reach] = cross
        piece[:, reach:] = side


def gradient_kernel(share, peers, aways, spots, other, where, *refs):
    count = peers * (1 + max(group for group, _ in spots))
    sources, refs = refs[:count], refs[count:]
    every_row, every_scored, lout_in, gram_in, grad_value, grad_out = refs[:6]
    tokens, x, slopes, normed, back, lout, gram, sems = refs[6:]
    first, dp_at, mp_at = where[0] == 1, where[1], where[2]
    take_row = jnp.logical_not(first) if other else first
    keep = share * peers
    width, inner, block = x.shape[1], lout.shape[0], gram.shape[1]
    piece = inner + block + SIDE
    copies = []

    def begin(source, target):
        copies.append(start_copy(source, target, sems.at[len(copies)]))

    ready = []
    for number, (away, (group, place)) in enumerate(zip(aways, spots)):
        start = number * keep
        here = pl.ds(pl.multiple_of((dp_at ^ away) * keep, keep), keep)
        target, sem = x.at[pl.ds(start, keep), :], sems.at[len(copies)]
        scored = every_scored.at[here, :]
        fetch(take_row, every_row.at[here, pl.ds(0, width)], scored, target, sem)
        copies.append(pltpu.make_async_copy(scored, target, sem))
        for mask in range(peers):
            at = pl.multiple_of(start + (mp_at ^ mask) * share, share)
            source = sources[group * peers + mask].at[:, pl.ds(place * piece, piece)]
            begin(source, tokens.at[pl.ds(at, share), :])
        ready.append(len(copies))
        if number == min(1, len(aways) - 1):
            maps = len(copies)
            begin(gram_in, gram)
            begin(lout_in, lout)
    done, step = 0, 2 if len(aways) % 2 == 0 else 1
    for number in range(0, len(aways), step):
        until = ready[number + step - 1]
        for index in range(done, until):
            if index not in (maps, maps + 1):
                copies[index].wait()
        done = until
        here = pl.ds(keep * number, keep * step)
        wide = x[here, :].astype(F32)
        side = tokens[here, inner + block :]
        portion = 1.0 / from_side(side, 1)
        normed[here, :] = (wide * from_side(side)).astype(BF)
        values = tokens[here, :inner]
        crossed = tokens[here, inner : inner + block].astype(F32)
        if number == 0:
            copies[maps].wait()
        back[here, :] = ((crossed + matmul(values, gram[...])) * portion).astype(BF)
        if number == 0:
            copies[maps + 1].wait()
        slopes[here, :] = ((wide + matmul(values, lout[...])) * portion).astype(BF)
    column = pl.ds(pl.multiple_of(dp_at * block, block), block)
    grad_value[...] = matmul_tn(back[...], normed[...]).astype(grad_value.dtype)
    grad_out[...] = matmul_tn(tokens[:, column], slopes[...]).astype(grad_out.dtype)


def add_kernel(value_near, out_near, value_far, out_far, grad_value, grad_out):
    grad_value[...] = value_near[...] + value_far[...].astype(F32)
    grad_out[...] = out_near[...] + out_far[...].astype(F32)


def square_sum(value):
    wide = value.astype(F32)
    return jnp.sum(wide * wide, axis=1, keepdims=True)


def exchange(first, second, first_mask, second_mask):
    first, second = lax.optimization_barrier((first, second))
    return lax.optimization_barrier(
        (flip(first, "mp", first_mask), flip(second, "mp", second_mask))
    )


def on_device(
    candidates,
    scorer_value,
    scorer_out,
    learner_value,
    learner_out,
    keep_index,
    keep_dest,
    keep_count,
):
    first = lax.axis_index("segment") == 0
    dp_at = lax.axis_index("dp")
    mp_at = lax.axis_index("mp")
    dp_size = lax.axis_size("dp")
    mp_size = lax.axis_size("mp")
    keep = keep_index.shape[1]
    width = candidates.shape[1]
    scorer_width = width * mp_size
    learner_width = 2 * scorer_width
    inner = learner_value.shape[2]
    block = inner // dp_size
    share = keep // mp_size

    own_value, own_out = scorer_value[0], scorer_out[0]
    own_lvalue, own_lout = learner_value[0], learner_out[0]
    other_value = flip(own_value, "segment", 1)

    is_live = jnp.arange(keep) < keep_count[0]
    pick = (keep_index[0][:, None] == jnp.arange(candidates.shape[0])[None, :]) & is_live[:, None]
    rows = matmul(pick.astype(BF), candidates).astype(BF)
    goal = jnp.where(is_live, keep_dest[0] + 1, 0).astype(F32)[:, None]
    rows_wide = jnp.concatenate([rows, jnp.broadcast_to(goal, (keep, SIDE)).astype(BF)], axis=1)

    gram = matmul_nt(own_lout, lax.dynamic_slice_in_dim(own_lout, dp_at * block, block, 0))
    half = inner // 2
    at = lax.axis_index("segment")
    kept_half = lax.dynamic_slice_in_dim(gram, at * half, half, 0)
    sent_half = lax.dynamic_slice_in_dim(gram, (1 - at) * half, half, 0)
    got_half = flip(sent_half.astype(BF), "segment", 1)

    direct = dp_size <= 8 and block % SIDE == 0
    flag = first.astype(jnp.int32)
    half_rows = keep // 2
    sums = [jax.ShapeDtypeStruct((keep, inner), F32), jax.ShapeDtypeStruct((keep, 1), F32)]
    state = sums + [jax.ShapeDtypeStruct((half_rows, inner + SIDE), BF)] * 2
    wide_state = state
    if direct:
        extra = half * block // keep
        wide_state = sums + [jax.ShapeDtypeStruct((half_rows, inner + SIDE + extra), BF)] * 2
        wide_state.append(jax.ShapeDtypeStruct((half, block), F32))
    hidden_type = jax.ShapeDtypeStruct((keep, width), BF)
    where = jnp.stack([flag, mp_at, dp_at])
    weight = pltpu.VMEM(own_value.shape, BF)

    def placed(*arrays):
        return [pltpu.with_memory_space_constraint(array, pltpu.HBM) for array in arrays]

    def halves(outs):
        return outs[0], outs[1], outs[2:4], list(outs[4:])

    *outs, repeated = call(
        functools.partial(start_kernel, direct),
        wide_state + [pltpu.HBM((dp_size * keep, width + SIDE), BF)],
        [SMEM, VMEM, HBM, HBM] + [VMEM] * (2 * direct),
        [weight, pltpu.SemaphoreType.DMA, pltpu.SemaphoreType.DMA((dp_size,))],
        mebibytes=12,
        out_specs=[VMEM] * len(wide_state) + [HBM],
    )(
        where,
        rows_wide,
        *placed(own_value, other_value),
        *((kept_half, got_half) if direct else ()),
    )
    part, rows_squares, sents, gram_sum = halves(outs)
    every_row = lax.all_to_all(repeated, "dp", 0, 0, tiled=True)
    own_out, own_lvalue, own_lout, sents = lax.optimization_barrier(
        (own_out, own_lvalue, own_lout, sents)
    )
    other_out = flip(own_out, "segment", 1)
    other_lvalue = flip(own_lvalue, "segment", 1)
    other_lout = flip(own_lout, "segment", 1)
    got = exchange(*sents, 1, 2)
    outs = call(
        functools.partial(between_kernel, direct), wide_state, [VMEM] * (4 + direct), mebibytes=8
    )(part, rows_squares, *got, *gram_sum)
    part, norm, sents, gram_sum = halves(outs)
    got = exchange(*sents, 2, 1)
    outs = call(
        functools.partial(section_kernel, scorer_width, direct),
        [hidden_type] + state + [jax.ShapeDtypeStruct((half, block), BF)] * direct,
        [SMEM] + [VMEM] * 5 + [HBM] * 4 + [VMEM] * direct,
        [weight, weight, pltpu.SemaphoreType.DMA((2,))],
        mebibytes=12,
    )(where, part, norm, *got, rows, *placed(own_out, other_out, own_value, other_value), *gram_sum)
    middle, outs = outs[0], outs[1:]
    part, norm, sents, gram_sum = halves(outs)
    learner_weights = placed(own_lvalue, other_lvalue, own_lout, other_lout)
    given = call(
        learn_kernel,
        [jax.ShapeDtypeStruct((keep, 2 * inner), F32)],
        [SMEM, VMEM] + [HBM] * 4,
        [weight, weight, pltpu.SemaphoreType.DMA((2,))],
        mebibytes=10,
    )(where, rows, *learner_weights)[0]
    got = exchange(*sents, 1, 2)
    outs = call(functools.partial(between_kernel, False), state, [VMEM] * 4)(part, norm, *got)
    part, norm, sents, _ = halves(outs)
    sents, given = lax.optimization_barrier((sents, given))
    got = exchange(*sents, 2, 1)

    long = 2 * inner + SIDE
    scored, norm, repeated = call(
        functools.partial(score_kernel, scorer_width),
        [hidden_type, sums[1], pltpu.HBM((dp_size * keep, width), BF)],
        [SMEM] + [VMEM] * 6 + [HBM] * 2,
        [weight, pltpu.SemaphoreType.DMA((dp_size + 1,))],
        mebibytes=10,
        out_specs=[VMEM, VMEM, HBM],
    )(
        where,
        part,
        norm,
        *got,
        middle,
        rows_squares,
        *placed(own_out, other_out),
    )
    every_scored = lax.all_to_all(repeated, "dp", 0, 0, tiled=True)
    outs = call(
        functools.partial(share_kernel, share),
        [
            jax.ShapeDtypeStruct((share, 2 * inner), F32),
            jax.ShapeDtypeStruct((share, 1), F32),
            jax.ShapeDtypeStruct((share, 1), F32),
        ]
        + [pltpu.HBM((share, long), BF)] * (mp_size - 1),
        [SMEM] + [VMEM] * 3 + [HBM] * 5,
        [
            weight,
            weight,
            pltpu.VMEM((keep, 2 * inner), F32),
            pltpu.VMEM((keep, long), BF),
            pltpu.VMEM((dp_size * keep, SIDE), BF),
            pltpu.SemaphoreType.DMA((mp_size + 2,)),
        ],
        mebibytes=12,
        out_specs=[VMEM] * 3 + [HBM] * (mp_size - 1),
    )(where, scored, norm, given, *learner_weights, every_row)
    kept, kept_norm, shard_count = outs[:3]

    got = lax.optimization_barrier(
        tuple(flip(peer, "mp", mask) for mask, peer in enumerate(outs[3:], 1))
    )
    pieces = call(
        functools.partial(value_kernel, learner_width, block, mp_size - 1),
        [jax.ShapeDtypeStruct((share, inner + block + SIDE), BF)] * dp_size
        if direct
        else [jax.ShapeDtypeStruct((share, long), BF)],
        [SMEM] + [VMEM] * (mp_size + 2),
        [pltpu.VMEM((share, inner), BF)],
    )(jnp.stack([dp_at]), kept, kept_norm, shard_count, *got)

    if direct:
        gram_half = gram_sum[0]
    else:
        gram_half = lax.psum(kept_half + got_half.astype(F32), "mp").astype(BF)
    gram_other = flip(gram_half, "segment", 1)
    gram = jnp.where(
        first,
        jnp.concatenate([gram_half, gram_other], axis=0),
        jnp.concatenate([gram_other, gram_half], axis=0),
    )

    column = dp_at * block

    def spread(piece):
        whole = jnp.zeros((keep, piece.shape[1]), BF)
        for mask in range(mp_size):
            got = flip(piece, "mp", mask) if mask else piece
            whole = lax.dynamic_update_slice(whole, got, ((mp_at ^ mask) * share, 0))
        return whole

    def add(grads, tokens, place):
        v = tokens[:, :inner]
        xo = tokens[:, inner : inner + block].astype(F32)
        inv = unpack(tokens[:, inner + block :], 0)
        share_count = 1.0 / unpack(tokens[:, inner + block :], 1)
        back = ((xo + matmul(v, gram)) * share_count).astype(BF)
        v_block = lax.dynamic_slice_in_dim(v, column, block, 1)
        row = lax.dynamic_slice(every_row, (place * keep, 0), (keep, width))
        score = lax.dynamic_slice_in_dim(every_scored, place * keep, keep, 0)
        added = []
        for x, lout in (
            (jnp.where(first, row, score), own_lout),
            (jnp.where(first, score, row), other_lout),
        ):
            x = x.astype(F32)
            slopes = ((x + matmul(v, lout)) * share_count).astype(BF)
            normed = (x * inv).astype(BF)
            added += [matmul_tn(back, normed), matmul_tn(v_block, slopes)]
        return [grad + new for grad, new in zip(grads, added)]

    if direct:
        moved = [flip(pieces[away], "dp", away) for away in range(1, dp_size)]
        soon = min(3, mp_size)
        own = [pieces[0]] + [flip(pieces[0], "mp", mask) for mask in range(1, soon)]
        moved, own, diagonal = lax.optimization_barrier((moved, own, pieces[0]))
        own += [flip(diagonal, "mp", mask) for mask in range(soon, mp_size)]
        rest = jnp.concatenate(moved, axis=1) if moved else None
        places_at = jnp.stack([flag, dp_at, mp_at])

        def gradients(aways, spots, groups, inputs, other, kind):
            tokens = len(aways) * keep
            return call(
                functools.partial(gradient_kernel, share, mp_size, aways, spots, other),
                [jax.ShapeDtypeStruct((block, width), kind)] * 2,
                [SMEM] + [HBM] * (len(groups) + 4),
                [
                    pltpu.VMEM((tokens, inner + block + SIDE), BF),
                    pltpu.VMEM((tokens, width), BF),
                    pltpu.VMEM((tokens, width), BF),
                    pltpu.VMEM((tokens, width), BF),
                    pltpu.VMEM((tokens, block), BF),
                    pltpu.VMEM(own_lout.shape, BF),
                    pltpu.VMEM(gram.shape, BF),
                    pltpu.SemaphoreType.DMA((len(aways) * (mp_size + 1) + 2,)),
                ],
                mebibytes=16,
            )(places_at, *groups, *placed(*inputs, other_lout if other else own_lout, gram))

        groups, spots = own, ((0, 0),)
        if dp_size > 1:
            groups = own + [rest] + [flip(rest, "mp", mask) for mask in range(1, mp_size)]
            spots += tuple((1, place) for place in range(dp_size - 1))
        inputs = (every_row, every_scored)
        aways = tuple(range(dp_size))
        far = gradients(aways, spots, groups, inputs, True, BF)
        near = gradients(aways, spots, groups, inputs, False, F32)
    else:
        ring = [(source, (source + 1) % dp_size) for source in range(dp_size)]

        def turn(step, carry):
            grads, full = carry
            cross = lax.dynamic_slice_in_dim(full, inner + column, block, 1)
            piece = jnp.concatenate([full[:, :inner], cross, full[:, 2 * inner :]], axis=1)
            grads = add(grads, spread(piece), (dp_at - step) % dp_size)
            return grads, lax.ppermute(full, "dp", ring)

        grads = [jnp.zeros((block, width), F32)] * 4
        grads, _ = lax.fori_loop(0, dp_size, turn, (grads, pieces[0]))
        near, far = grads[:2], [grad.astype(BF) for grad in grads[2:]]
    got = [flip(sent, "segment", 1) for sent in far]
    grads = call(
        add_kernel,
        [jax.ShapeDtypeStruct((block, width), F32)] * 2,
        [VMEM] * 4,
        mebibytes=10,
    )(*near, *got)
    return (grads[0][None], grads[1][None])


def solution(mesh):
    placed = (
        P(("segment", "dp"), "mp"),
        P("segment", "mp", None),
        P("segment", None, "mp"),
        P("segment", "mp", None),
        P("segment", None, "mp"),
        P(("segment", "dp"), None),
        P(("segment", "dp"), None),
        P(("segment", "dp")),
    )
    return jax.shard_map(
        on_device,
        mesh=mesh,
        in_specs=placed,
        out_specs=(P("segment", "dp", "mp"), P("segment", "dp", "mp")),
        check_vma=False,
    )
```
